32 devices in a mesh: segment: 2 (over core), seq: 8 (over z, y), tp: 2 (over x).
Axes of the slice: x: 2, y: 2, z: 4, core: 2. Of those that a mesh axis runs over, the one named last changes fastest.
Arguments:
- inputs: bfloat16 [2, 2048, 2688], P(None, 'seq', 'tp'), may hold values from -6 to 6
- lengths: int32 [2, 8], replicated, may hold values from 64 to 256
- boundary: int32 [2], replicated, may hold values from 0 to 2047
- attn_gain: float32 [2, 2688], P('segment'), may hold values from 0.5 to 1.5
- query_weight: bfloat16 [2, 2688, 2048], P('segment', 'seq', 'tp')
- key_weight: bfloat16 [2, 2688, 1024], P('segment', None, 'tp')
- value_weight: bfloat16 [2, 2688, 1024], P('segment', None, 'tp'), may hold values from -0.125 to 0.125
- out_weight: bfloat16 [2, 2048, 2688], P('segment', 'tp', 'seq'), may hold values from -0.125 to 0.125
Outputs:
- layer_states: bfloat16 [2, 2, 2048, 2688], P('segment', None, 'seq', 'tp')
The draws below stay inside these ranges and needn't reach their ends.
All inputs are finite; a program needn't handle non-finite values.
Results may differ from the reference program's by a relative error of at most 0.02.
Values may be sent and summed in bfloat16 or wider, within the bound.
No kernel may reach another device: no remote copies, remote signals or barrier semaphores. Data moves between devices by JAX's collectives and lax.ppermute only.
A program may use at most 128 MiB of HBM per device.

```python
import math
import jax
import jax.numpy as jnp
from jax import lax

D = 2688
HEADS = 16
KV = 8
HEAD_DIM = 128
WINDOW = 1024
BLOCK = 256
BATCH = 2
LAYERS = 2
TOKENS = 2048
N_SEQ = 8


def query_matrix(key):
    return jax.random.normal(jax.random.fold_in(key, 11), (LAYERS, D, HEADS * HEAD_DIM), jnp.float32) * D ** (-0.5)


def draw_query_weight(key, part):
    return query_matrix(key).astype(jnp.bfloat16)


def draw_key_weight(key, part):
    return (jax.random.normal(jax.random.fold_in(key, 17), (LAYERS, D, KV * HEAD_DIM), jnp.float32) * D ** (-0.5)).astype(jnp.bfloat16)


def plant(values, rng, smallest, top_value):
    place = [jax.random.randint(jax.random.fold_in(rng, axis), (), 0, length) for axis, length in enumerate(values.shape)]
    longest = values.shape.index(max(values.shape))
    beside = place[:longest] + [(place[longest] + 1) % values.shape[longest]] + place[longest + 1:]
    return values.at[tuple(place)].set(smallest).at[tuple(beside)].set(top_value)


def steps_of(rng, dims, shards, low, top_value):
    level, own = 1.0, jax.random.fold_in(rng, 6)
    for dim, blocks in shards:
        heights = jnp.exp(jax.random.uniform(jax.random.fold_in(own, dim), (blocks,), jnp.float32, low / len(shards), top_value / len(shards)))
        level = level * jnp.repeat(heights, dims[dim] // blocks).reshape([-1 if axis == dim else 1 for axis in range(len(dims))])
    return level


def noise(key, shape, scale, most, cuts=(), held_as=jnp.bfloat16):
    gain = steps_of(key, shape, cuts, -0.22, 0.18) if cuts else 1.0
    drawn = jax.random.normal(key, shape, jnp.float32) * scale * gain
    return jnp.minimum(jnp.maximum(drawn, -most), most).astype(held_as)


def setup_inputs(seed: int = 0) -> dict:
    key_list = jax.random.split(jax.random.key(seed), 9)
    inputs = noise(key_list[0], (BATCH, TOKENS, D), 1.0, 6.0, ((1, 8), (2, 2)))
    lengths = plant(jax.random.randint(key_list[1], (BATCH, N_SEQ), BLOCK // 4, BLOCK + 1), jax.random.fold_in(key_list[1], 1), BLOCK // 4, BLOCK).astype(jnp.int32)
    boundary = jax.random.randint(key_list[2], (BATCH,), 0, TOKENS).astype(jnp.int32)
    attn_gain = jnp.clip(1.0 + 0.1 * jax.random.normal(key_list[3], (LAYERS, D), jnp.float32), 0.5, 1.5)
    query_weight = draw_query_weight(jax.random.fold_in(key_list[8], 71), 0)
    key_weight = draw_key_weight(jax.random.fold_in(key_list[8], 71), 0)
    value_weight = noise(key_list[6], (LAYERS, D, KV * HEAD_DIM), D ** -0.5, 0.125, ((0, 2), (2, 2)))
    out_weight = noise(key_list[7], (LAYERS, HEADS * HEAD_DIM, D), (HEADS * HEAD_DIM) ** -0.5, 0.125, ((0, 2), (1, 2), (2, 8)))
    return dict(inputs=inputs, lengths=lengths, boundary=boundary, attn_gain=attn_gain, query_weight=query_weight, key_weight=key_weight, value_weight=value_weight, out_weight=out_weight)


norm_epsilon = 1e-06

def normalize(state, norm_gain):
    widened = state.astype(jnp.float32)
    mean_square = lax.optimization_barrier(jnp.mean(widened * widened, axis=-1, keepdims=True))
    return (widened * lax.rsqrt(mean_square + norm_epsilon) * norm_gain).astype(jnp.bfloat16)

def rotate(tensor, positions):
    half_dim = tensor.shape[-1] // 2
    inverse = jnp.exp(-math.log(10000.0) * jnp.arange(half_dim, dtype=jnp.float32) * (2.0 / tensor.shape[-1]))
    angles = positions.astype(jnp.float32)[:, None] * inverse[None, :]
    cosine = jnp.cos(angles)[:, None, :]
    sine_part = jnp.sin(angles)[:, None, :]
    first_half = tensor[..., :half_dim]
    second_half = tensor[..., half_dim:]
    return jnp.concatenate([first_half * cosine - second_half * sine_part, second_half * cosine + first_half * sine_part], axis=-1)

def reference(inputs, lengths, boundary, attn_gain, query_weight, key_weight, value_weight, out_weight):
    batch_count = inputs.shape[0]
    seq_blocks = TOKENS // BLOCK
    reach_blocks = max(1, WINDOW // BLOCK)
    group_size = HEADS // KV
    front = reach_blocks * BLOCK
    slots = jnp.arange(TOKENS, dtype=jnp.int32)
    slot_valid = (slots % BLOCK)[None, :] < jnp.repeat(lengths, BLOCK, axis=1)
    padded_valid = jnp.concatenate([jnp.zeros((batch_count, front), dtype=bool), slot_valid], axis=1)
    state = inputs
    outputs = []
    for layer_index in range(LAYERS):
        normed = normalize(state, attn_gain[layer_index])
        flat = normed.reshape(-1, D)
        queries = jnp.dot(flat, query_weight[layer_index], preferred_element_type=jnp.float32)
        queries = rotate(queries.reshape(batch_count, TOKENS, HEADS, HEAD_DIM), slots).astype(jnp.bfloat16)
        key_rows = jnp.dot(flat, key_weight[layer_index], preferred_element_type=jnp.float32)
        key_rows = rotate(key_rows.reshape(batch_count, TOKENS, KV, HEAD_DIM), slots).astype(jnp.bfloat16)
        value_rows = jnp.dot(flat, value_weight[layer_index], preferred_element_type=jnp.float32).astype(jnp.bfloat16)
        value_rows = value_rows.reshape(batch_count, TOKENS, KV, HEAD_DIM)
        zero_front = jnp.zeros((batch_count, front, KV, HEAD_DIM), jnp.bfloat16)
        key_padded = jnp.concatenate([zero_front, key_rows], axis=1)
        value_padded = jnp.concatenate([zero_front, value_rows], axis=1)

        def one_block(block_id):
            start = (block_id * BLOCK).astype(jnp.int32)
            query_block = lax.dynamic_slice_in_dim(queries, start, BLOCK, 1).reshape(batch_count, BLOCK, KV, group_size, HEAD_DIM)
            key_block = lax.dynamic_slice_in_dim(key_padded, start, front + BLOCK, 1)
            value_block = lax.dynamic_slice_in_dim(value_padded, start, front + BLOCK, 1)
            key_valid = lax.dynamic_slice_in_dim(padded_valid, start, front + BLOCK, 1)
            query_valid = lax.dynamic_slice_in_dim(slot_valid, start, BLOCK, 1)
            query_slots = start + jnp.arange(BLOCK, dtype=jnp.int32)
            key_slots = start - front + jnp.arange(front + BLOCK, dtype=jnp.int32)
            inside = (key_slots[None, :] <= query_slots[:, None]) & (key_slots[None, :] > query_slots[:, None] - WINDOW)
            episode = (query_slots[None, :, None] < boundary[:, None, None]) | (key_slots[None, None, :] >= boundary[:, None, None])
            visible = inside[None] & key_valid[:, None, :] & query_valid[:, :, None] & episode
            scores = jnp.einsum('bqgjd,bkgd->bgjqk', query_block.astype(jnp.float32), key_block.astype(jnp.float32)) * HEAD_DIM ** (-0.5)
            seen = visible[:, None, None]
            masked = jnp.where(seen, scores, -1e+30)
            row_max = lax.optimization_barrier(jnp.max(masked, axis=-1, keepdims=True))
            exp_terms = jnp.where(seen, jnp.exp(masked - row_max), 0.0)
            row_total = lax.optimization_barrier(jnp.sum(exp_terms, axis=-1, keepdims=True))
            row_total = jnp.where(query_valid[:, None, None, :, None], row_total, 1.0)
            weights = (exp_terms / row_total).astype(jnp.bfloat16)
            mixed_heads = jnp.einsum('bgjqk,bkgd->bqgjd', weights.astype(jnp.float32), value_block.astype(jnp.float32)).astype(jnp.bfloat16)
            return mixed_heads.reshape(batch_count, BLOCK, HEADS * HEAD_DIM)
        blocks = lax.map(one_block, jnp.arange(seq_blocks, dtype=jnp.int32))
        attended = jnp.transpose(blocks, (1, 0, 2, 3)).reshape(batch_count * TOKENS, HEADS * HEAD_DIM)
        update = jnp.dot(attended, out_weight[layer_index], preferred_element_type=jnp.float32).reshape(batch_count, TOKENS, D)
        state = (state.astype(jnp.float32) + update).astype(jnp.bfloat16)
        outputs.append(state)
    return jnp.stack(outputs)
```

```python
import functools
import math

import jax
import jax.numpy as jnp
from jax import lax
from jax.experimental import pallas as pl
from jax.experimental.pallas import tpu as pltpu
from jax.sharding import PartitionSpec as P

HEADS = 16
KV = 8
HEAD_DIM = 128
WINDOW = 1024
GROUP = HEADS // KV
LAYERS = 2

norm_epsilon = 1e-06
hidden = -1e30
VMEM_LIMIT = 48 * 1024 * 1024

SWAP = ((0, 1), (1, 0))


def ring_order(count):
    return list(range(0, count, 2)) + list(range(count - 1, 0, -2))


def ring_position(index, count):
    return jnp.where(index % 2 == 0, index // 2, count - 1 - index // 2)


def ring_member(position, count):
    position = lax.rem(position + 2 * count, count)
    return jnp.where(position < count // 2, 2 * position, 2 * (count - 1 - position) + 1)


def any_spec():
    return pl.BlockSpec(memory_space=pl.ANY)


def vmem_spec():
    return pl.BlockSpec(memory_space=pltpu.VMEM)


def smem_spec():
    return pl.BlockSpec(memory_space=pltpu.SMEM)


def call(kernel, out_shape, in_specs, scratch, flops, moved, name, exps=0):
    outs = jax.tree.map(lambda _: vmem_spec(), out_shape)
    return pl.pallas_call(
        kernel,
        out_shape=out_shape,
        in_specs=in_specs,
        out_specs=outs,
        scratch_shapes=scratch,
        compiler_params=pltpu.CompilerParams(vmem_limit_bytes=VMEM_LIMIT),
        cost_estimate=pl.CostEstimate(flops=flops, bytes_accessed=moved, transcendentals=exps),
        name=name,
    )


def turned(heads, cosine, sine):
    return heads * cosine + pltpu.roll(heads, HEAD_DIM // 2, 1) * sine


def key_value_kernel(
    layer, own, other, gain, cosine, sine, key_own, key_came, value_own, value_came,
    kv_out, normed_out, weights, normed, sems,
):
    here = lax.axis_index("segment") == layer
    half = lax.axis_index("tp")
    width = own.shape[1]
    columns = key_own.shape[1]
    step = 256 if columns % 256 == 0 else columns
    parts = columns // step

    def copies(key, value):
        made = []
        for which, source in enumerate((key, value)):
            for part in range(parts):
                made.append(
                    pltpu.make_async_copy(
                        source.at[:, pl.ds(part * step, step)],
                        weights.at[which * parts + part],
                        sems.at[which * parts + part],
                    )
                )
        return made

    @pl.when(here)
    def _():
        for copy in copies(key_own, value_own):
            copy.start()

    @pl.when(jnp.logical_not(here))
    def _():
        for copy in copies(key_came, value_came):
            copy.start()

    mine = own[...].astype(jnp.float32)
    theirs = other[...].astype(jnp.float32)
    total = jnp.sum(mine * mine, axis=1, keepdims=True)
    total += jnp.sum(theirs * theirs, axis=1, keepdims=True)
    scale = lax.rsqrt(total / (2 * width) + norm_epsilon)
    normed[0] = (mine * scale * gain[pl.ds(half, 1), :]).astype(jnp.bfloat16)
    normed[1] = (theirs * scale * gain[pl.ds(1 - half, 1), :]).astype(jnp.bfloat16)
    chunks = normed_out.shape[0] // 2
    depth = normed_out.shape[2]
    for part in range(chunks):
        normed_out[half * chunks + part] = normed[0, :, part * depth : (part + 1) * depth]
        normed_out[(1 - half) * chunks + part] = normed[1, :, part * depth : (part + 1) * depth]

    waits = copies(key_own, value_own)
    for index, copy in enumerate(waits):
        copy.wait()
        result = jnp.dot(
            normed[0],
            weights[index, pl.ds(pl.multiple_of(half * width, 16), width), :],
            preferred_element_type=jnp.float32,
        )
        result += jnp.dot(
            normed[1],
            weights[index, pl.ds(pl.multiple_of((1 - half) * width, 16), width), :],
            preferred_element_type=jnp.float32,
        )
        base = index * step
        if index < parts:
            for head in range(step // HEAD_DIM):
                rows = result[:, head * HEAD_DIM : (head + 1) * HEAD_DIM]
                kv_out[:, base + head * HEAD_DIM : base + (head + 1) * HEAD_DIM] = turned(
                    rows, cosine[...], sine[...]
                ).astype(jnp.bfloat16)
        else:
            kv_out[:, base : base + step] = result.astype(jnp.bfloat16)


def key_value(layer, own, other, gain, tables, weights, count):
    rows, width = own.shape
    depth, columns = weights[0].shape
    step = 256 if columns % 256 == 0 else columns
    parts = 2 * (columns // step)
    return call(
        functools.partial(key_value_kernel, layer),
        (
            jax.ShapeDtypeStruct((rows, 2 * columns), jnp.bfloat16),
            jax.ShapeDtypeStruct((count, rows, depth // count), jnp.bfloat16),
        ),
        [vmem_spec()] * 5 + [any_spec()] * 4,
        [
            pltpu.VMEM((parts, depth, step), jnp.bfloat16),
            pltpu.VMEM((2, rows, width), jnp.bfloat16),
            pltpu.SemaphoreType.DMA((parts,)),
        ],
        4 * rows * depth * columns,
        4 * depth * columns + 4 * rows * depth,
        "key_value",
    )(own, other, gain, *tables, *weights)


def piece_copy(ref, part, target, sem):
    source = ref.at[part] if ref.shape[0] > 1 else ref.at[0]
    return pltpu.make_async_copy(source, target, sem)


def query_kernel(count, normed, cosine, sine, *refs):
    pieces, (out, weights, sems) = refs[: 2 * count], refs[2 * count :]
    core = lax.axis_index("segment")
    place = ring_position(lax.axis_index("seq"), count)
    copies = [
        piece_copy(piece, 0, weights.at[index], sems.at[index])
        for index, piece in enumerate(pieces)
    ]
    for copy in copies:
        copy.start()
    for side in range(2):
        total = None
        for step in range(count):
            index = side * count + step
            copies[index].wait()
            term = jnp.dot(
                normed[ring_member(place - step, count)],
                weights[index],
                preferred_element_type=jnp.float32,
            )
            total = term if total is None else total + term
        target = core if side == 0 else 1 - core
        for head in range(total.shape[1] // HEAD_DIM):
            cut = slice(head * HEAD_DIM, (head + 1) * HEAD_DIM)
            out[target, :, cut] = turned(total[:, cut], cosine[...], sine[...]).astype(
                jnp.bfloat16
            )


def query(normed, tables, own, came):
    count, rows, depth = normed.shape
    columns = own[0].shape[2]
    return call(
        functools.partial(query_kernel, count),
        jax.ShapeDtypeStruct((2, rows, columns), jnp.bfloat16),
        [vmem_spec()] * 3 + [any_spec()] * (2 * count),
        [
            pltpu.VMEM((2 * count, depth, columns), jnp.bfloat16),
            pltpu.SemaphoreType.DMA((2 * count,)),
        ],
        4 * count * rows * depth * columns,
        4 * count * depth * columns + 2 * count * rows * depth,
        "query",
    )(normed, *tables, *own, *came)


def attend_kernel(reach, lengths, boundary, queries, *refs):
    windows, (out, bias) = refs[: reach + 1], refs[reach + 1 :]
    batch = lax.axis_index("segment")
    seq = lax.axis_index("seq")
    rows = queries.shape[1]
    half_heads = queries.shape[2] // HEAD_DIM
    kv_columns = windows[0].shape[1] // 2
    row_ids = lax.broadcasted_iota(jnp.int32, (rows, rows), 0)
    key_ids = lax.broadcasted_iota(jnp.int32, (rows, rows), 1)
    start = boundary[batch]
    for slot in range(reach + 1):
        distance = reach - slot
        block = seq - distance
        length = jnp.where(block >= 0, lengths[batch, jnp.maximum(block, 0)], 0)
        seen = key_ids < length
        if distance == 0:
            seen &= key_ids <= row_ids
        if distance == reach:
            seen &= key_ids > row_ids + (distance * rows - WINDOW)
        seen &= (row_ids + seq * rows < start) | (key_ids + block * rows >= start)
        bias[slot] = jnp.where(seen, 0.0, hidden)
    own_length = lengths[batch, seq]
    kept = lax.broadcasted_iota(jnp.int32, (rows, 1), 0) < own_length
    factor = math.log2(math.e) * HEAD_DIM ** (-0.5)
    for head in range(2 * half_heads):
        group = head // GROUP
        cut = slice(group * HEAD_DIM, (group + 1) * HEAD_DIM)
        value_cut = slice(kv_columns + group * HEAD_DIM, kv_columns + (group + 1) * HEAD_DIM)
        half, place = head // half_heads, head % half_heads
        query_rows = queries[half, :, place * HEAD_DIM : (place + 1) * HEAD_DIM]
        scores = [
            lax.dot_general(
                query_rows,
                windows[slot][:, cut],
                (((1,), (1,)), ((), ())),
                preferred_element_type=jnp.float32,
            )
            + bias[slot]
            for slot in range(reach + 1)
        ]
        top = scores[0]
        for score in scores[1:]:
            top = jnp.maximum(top, score)
        top = jnp.max(top, axis=1, keepdims=True)
        mixed = None
        total = None
        for slot in range(reach + 1):
            term = jnp.exp2((scores[slot] - top) * factor)
            total = term if total is None else total + term
            product = jnp.dot(
                term.astype(jnp.bfloat16),
                windows[slot][:, value_cut],
                preferred_element_type=jnp.float32,
            )
            mixed = product if mixed is None else mixed + product
        total = jnp.sum(total, axis=1, keepdims=True)
        result = jnp.where(kept, mixed / total, 0.0)
        out[half, :, place * HEAD_DIM : (place + 1) * HEAD_DIM] = result.astype(jnp.bfloat16)


def attend(lengths, boundary, queries, windows):
    reach = len(windows) - 1
    rows = queries.shape[1]
    heads = 2 * queries.shape[2] // HEAD_DIM
    keys = rows * len(windows)
    return call(
        functools.partial(attend_kernel, reach),
        jax.ShapeDtypeStruct(queries.shape, jnp.bfloat16),
        [smem_spec()] * 2 + [vmem_spec()] * (reach + 2),
        [pltpu.VMEM((reach + 1, rows, rows), jnp.float32)],
        4 * heads * rows * keys * HEAD_DIM,
        2 * sum(w.size for w in windows) + 4 * queries.size,
        "attend",
        heads * rows * keys,
    )(lengths, boundary, queries, *windows)


def out_kernel(count, mixed, *refs):
    pieces, (leave, stay, weights, chunks, sems) = refs[: 2 * count], refs[2 * count :]
    core = lax.axis_index("segment")
    half = lax.axis_index("tp")
    place = ring_position(lax.axis_index("seq"), count)
    copies = [
        piece_copy(piece, 1, weights.at[index], sems.at[index])
        for index, piece in enumerate(pieces)
    ]
    for step in range(count):
        copies[step].start()
        copies[count + step].start()
    contract = (((1,), (1,)), ((), ()))
    for step in range(count):
        copies[step].wait()
        copies[count + step].wait()
        result = lax.dot_general(
            mixed[core], weights[step], contract, preferred_element_type=jnp.float32
        )
        result += lax.dot_general(
            mixed[1 - core], weights[count + step], contract, preferred_element_type=jnp.float32
        )
        chunks[ring_member(place - step, count)] = result
    parts = count // 2
    width = chunks.shape[2]
    for part in range(parts):
        cut = slice(part * width, (part + 1) * width)
        stay[:, cut] = chunks[half * parts + part]
        leave[:, cut] = chunks[(1 - half) * parts + part].astype(jnp.bfloat16)


def out_project(mixed, own, came):
    count = len(own)
    rows, columns = mixed.shape[1:]
    depth = own[0].shape[1]
    width = count // 2 * depth
    return call(
        functools.partial(out_kernel, count),
        (
            jax.ShapeDtypeStruct((rows, width), jnp.bfloat16),
            jax.ShapeDtypeStruct((rows, width), jnp.float32),
        ),
        [vmem_spec()] + [any_spec()] * (2 * count),
        [
            pltpu.VMEM((2 * count, depth, columns), jnp.bfloat16),
            pltpu.VMEM((count, rows, depth), jnp.float32),
            pltpu.SemaphoreType.DMA((2 * count,)),
        ],
        4 * count * rows * depth * columns,
        4 * count * depth * columns + 6 * rows * width,
        "out_project",
    )(mixed, *own, *came)


def after(value, *others):
    return lax.optimization_barrier((value, *others))[0]


def per_device(
    inputs, lengths, boundary, attn_gain, query_weight, key_weight, value_weight, out_weight
):
    core = lax.axis_index("segment")
    seq_index = lax.axis_index("seq")
    count = lax.axis_size("seq")
    block_len = inputs.shape[1]
    first_core = core == 0

    def across_chip(value):
        return lax.ppermute(value, "segment", SWAP)

    def across_tp(value):
        return lax.ppermute(value, "tp", SWAP)

    state = lax.dynamic_index_in_dim(inputs, core, 0, keepdims=False)
    state_other = across_tp(state)

    columns = query_weight.shape[2] // 2
    both = jnp.stack([query_weight[0], out_weight[0].T])
    mine = lax.dynamic_slice_in_dim(both, core * columns, columns, 2)
    given = lax.dynamic_slice_in_dim(both, (1 - core) * columns, columns, 2)
    came = across_chip(given)
    shards = [jnp.where(first_core, mine, came), jnp.where(first_core, came, mine)]
    key_value_weights = (
        key_weight[0],
        across_chip(key_weight[0]),
        value_weight[0],
        across_chip(value_weight[0]),
    )
    gain_came = across_chip(attn_gain)
    gains = [
        jnp.where(first_core, attn_gain, gain_came).reshape(2, -1),
        jnp.where(first_core, gain_came, attn_gain).reshape(2, -1),
    ]

    half_dim = HEAD_DIM // 2
    inverse = jnp.exp(
        -math.log(10000.0) * jnp.arange(half_dim, dtype=jnp.float32) * (2.0 / HEAD_DIM)
    )
    slots = seq_index * block_len + jnp.arange(block_len, dtype=jnp.int32)
    angles = slots.astype(jnp.float32)[:, None] * inverse[None, :]
    cosine, sine = jnp.cos(angles), jnp.sin(angles)
    tables = (
        jnp.concatenate([cosine, cosine], axis=1),
        jnp.concatenate([-sine, sine], axis=1),
    )

    order = ring_order(count)
    onward = [(order[i], order[(i + 1) % count]) for i in range(count)]
    back = [(b, a) for a, b in onward]

    def gather(shard):
        forward = [shard]
        backward = [shard]
        for _ in range(count // 2 - 1):
            forward.append(lax.ppermute(forward[-1], "seq", onward))
            backward.append(lax.ppermute(backward[-1], "seq", back))
        far_query = lax.ppermute(forward[-1][:1], "seq", onward)
        far_out = lax.ppermute(backward[-1][1:], "seq", back)
        near = forward + [None] + backward[:0:-1]
        middle = count // 2
        query_own = near[:middle] + [far_query] + near[middle + 1 :]
        out_own = near[:middle] + [far_out] + near[middle + 1 :]
        near_came = [None if piece is None else across_chip(piece) for piece in near]
        query_came = near_came[:middle] + [across_chip(far_query)] + near_came[middle + 1 :]
        out_came = near_came[:middle] + [across_chip(far_out)] + near_came[middle + 1 :]
        return query_own, query_came, out_own, out_came

    up = [(i, i + 2) for i in range(count - 2)]
    beside = [(i, i ^ 1) for i in range(count)]
    even = seq_index % 2 == 0
    reach = max(1, WINDOW // block_len)

    def window(rows):
        evens = [rows]
        odds = []
        for _ in range(reach // 2):
            evens.append(lax.ppermute(evens[-1], "seq", up))
            odds.append(
                lax.ppermute(jnp.where(even, evens[-2], evens[-1]), "seq", beside)
            )
        blocks = []
        for distance in range(reach, -1, -1):
            blocks.append(evens[distance // 2] if distance % 2 == 0 else odds[distance // 2])
        return blocks

    pieces = gather(shards[0])
    states = []
    for layer in range(LAYERS):
        kv_rows, normed = key_value(
            layer, state, state_other, gains[layer], tables, key_value_weights, count
        )
        blocks = window(kv_rows)
        query_own, query_came, out_own, out_came = pieces
        queries = query(normed, tables, query_own, query_came)
        mixed = attend(lengths, boundary, queries, blocks)
        if layer + 1 < LAYERS:
            pieces = gather(after(shards[layer + 1], *blocks[:-1]))
        leave, stay = out_project(mixed, out_own, out_came)
        arrived = across_tp(leave)
        state = (
            state.astype(jnp.float32) + stay + arrived.astype(jnp.float32)
        ).astype(jnp.bfloat16)
        states.append(state)
        if layer + 1 < LAYERS:
            state_other = across_tp(state)

    first_came = lax.ppermute(states[0], "segment", [(1, 0)])
    last_came = lax.ppermute(states[1], "segment", [(0, 1)])
    return jnp.stack(
        [
            jnp.where(first_core, states[0], last_came),
            jnp.where(first_core, first_came, states[1]),
        ]
    )[None]


def solution(mesh):
    return jax.shard_map(
        per_device,
        mesh=mesh,
        in_specs=(
            P(None, "seq", "tp"),
            P(),
            P(),
            P("segment", None),
            P("segment", "seq", "tp"),
            P("segment", None, "tp"),
            P("segment", None, "tp"),
            P("segment", "tp", "seq"),
        ),
        out_specs=P("segment", None, "seq", "tp"),
        check_vma=False,
    )
```

```python
import functools
import math

import jax
import jax.numpy as jnp
from jax import lax
from jax.experimental import pallas as pl
from jax.experimental.pallas import tpu as pltpu
from jax.sharding import PartitionSpec as P

HEADS = 16
KV = 8
HEAD_DIM = 128
WINDOW = 1024
GROUP = HEADS // KV
LAYERS = 2

norm_epsilon = 1e-06
hidden = -1e30
VMEM_LIMIT = 16 * 1024 * 1024

SWAP = ((0, 1), (1, 0))


def ring_order(count):
    return list(range(0, count, 2)) + list(range(count - 1, 0, -2))


def ring_position(index, count):
    return jnp.where(index % 2 == 0, index // 2, count - 1 - index // 2)


def ring_member(position, count):
    position = lax.rem(position + 2 * count, count)
    return jnp.where(position < count // 2, 2 * position, 2 * (count - 1 - position) + 1)


def hbm_spec():
    return pl.BlockSpec(memory_space=pltpu.HBM)


def vmem_spec():
    return pl.BlockSpec(memory_space=pltpu.VMEM)


def smem_spec():
    return pl.BlockSpec(memory_space=pltpu.SMEM)


def call(kernel, out_shape, in_specs, scratch, flops, moved, name, exps=0):
    outs = jax.tree.map(lambda _: vmem_spec(), out_shape)
    return pl.pallas_call(
        kernel,
        out_shape=out_shape,
        in_specs=in_specs,
        out_specs=outs,
        scratch_shapes=scratch,
        compiler_params=pltpu.CompilerParams(vmem_limit_bytes=VMEM_LIMIT),
        cost_estimate=pl.CostEstimate(flops=flops, bytes_accessed=moved, transcendentals=exps),
        name=name,
    )


def turned(heads, cosine, sine):
    return heads * cosine + pltpu.roll(heads, HEAD_DIM // 2, 1) * sine


def norm_rows(own, other, gain, half):
    width, rows = own.shape
    total = jnp.zeros((1, rows), jnp.float32)
    for source in (own, other):
        wide = source[...].astype(jnp.float32)
        total += jnp.sum(wide * wide, axis=0, keepdims=True)
    scale = lax.rsqrt(total / (2 * width) + norm_epsilon).T
    return [
        (source[...].T.astype(jnp.float32) * scale * gain[pl.ds(which, 1), :]).astype(
            jnp.bfloat16
        )
        for source, which in ((own, half), (other, 1 - half))
    ]


def key_value_kernel(own, other, gain, tables, key, value, kv_out, normed, angles, sem):
    half = lax.axis_index("tp")
    width = own.shape[0]
    step = key.shape[1] // 2
    table_copy = pltpu.make_async_copy(tables, angles, sem)
    table_copy.start()
    normed[0], normed[1] = norm_rows(own, other, gain, half)
    table_copy.wait()
    for index in range(4):
        weight = (key, value)[index // 2]
        cut = slice(index % 2 * step, (index % 2 + 1) * step)
        result = jnp.dot(
            normed[0],
            weight[pl.ds(pl.multiple_of(half * width, 16), width), cut],
            preferred_element_type=jnp.float32,
        )
        result += jnp.dot(
            normed[1],
            weight[pl.ds(pl.multiple_of((1 - half) * width, 16), width), cut],
            preferred_element_type=jnp.float32,
        )
        if index < 2:
            for head in range(step // HEAD_DIM):
                cut = slice(head * HEAD_DIM, (head + 1) * HEAD_DIM)
                kv_out[index, :, cut] = turned(result[:, cut], angles[0], angles[1]).astype(
                    jnp.bfloat16
                )
        else:
            kv_out[index] = result.astype(jnp.bfloat16).T


def key_value(own, other, gain, tables, weights):
    width, rows = own.shape
    depth, columns = weights[0].shape
    step = columns // 2
    return call(
        key_value_kernel,
        jax.ShapeDtypeStruct((4, rows, step), jnp.bfloat16),
        [vmem_spec()] * 3 + [hbm_spec()] + [vmem_spec()] * 2,
        [
            pltpu.VMEM((2, rows, width), jnp.bfloat16),
            pltpu.VMEM(tables.shape, jnp.float32),
            pltpu.SemaphoreType.DMA(()),
        ],
        4 * rows * depth * columns,
        4 * depth * columns + 4 * rows * depth,
        "key_value",
    )(own, other, gain, tables, *weights)


def query_kernel(count, own, other, gain, tables, *refs):
    pieces, (out, normed, angles, sem) = refs[: 2 * count], refs[2 * count :]
    table_copy = pltpu.make_async_copy(tables, angles, sem)
    table_copy.start()
    core = lax.axis_index("segment")
    half = lax.axis_index("tp")
    place = ring_position(lax.axis_index("seq"), count)
    chunks, depth = count // 2, normed.shape[2]
    for rows, which in zip(norm_rows(own, other, gain, half), (half, 1 - half)):
        for part in range(chunks):
            normed[which * chunks + part] = rows[:, part * depth : (part + 1) * depth]
    table_copy.wait()
    for side in range(2):
        total = None
        for step in range(count):
            term = jnp.dot(
                normed[ring_member(place - step, count)],
                pieces[side * count + step][0],
                preferred_element_type=jnp.float32,
            )
            total = term if total is None else total + term
        target = core if side == 0 else 1 - core
        for head in range(total.shape[1] // HEAD_DIM):
            cut = slice(head * HEAD_DIM, (head + 1) * HEAD_DIM)
            rows = turned(total[:, cut], angles[0], angles[1]).astype(jnp.bfloat16)
            out[target, cut, :] = rows.T


def query(state, other, gain, tables, own, came):
    count = len(own)
    width, rows = state.shape
    depth, columns = own[0].shape[1:]
    return call(
        functools.partial(query_kernel, count),
        jax.ShapeDtypeStruct((2, columns, rows), jnp.bfloat16),
        [vmem_spec()] * 3 + [hbm_spec()] + [vmem_spec()] * (2 * count),
        [
            pltpu.VMEM((count, rows, depth), jnp.bfloat16),
            pltpu.VMEM(tables.shape, jnp.float32),
            pltpu.SemaphoreType.DMA(()),
        ],
        4 * count * rows * depth * columns,
        4 * count * depth * columns + 2 * count * rows * depth,
        "query",
    )(state, other, gain, tables, *own, *came)


def head_cuts(head, half_heads, groups):
    group = head // GROUP
    side, within = group // groups, group % groups
    cut = slice(within * HEAD_DIM, (within + 1) * HEAD_DIM)
    half, place = head // half_heads, head % half_heads
    return half, slice(place * HEAD_DIM, (place + 1) * HEAD_DIM), side, cut


def score_bias(distance, reach, rows, lengths, boundary):
    batch = lax.axis_index("segment")
    seq = lax.axis_index("seq")
    key_ids = lax.broadcasted_iota(jnp.int32, (rows, rows), 0)
    query_ids = lax.broadcasted_iota(jnp.int32, (rows, rows), 1)
    start = boundary[batch]
    block = seq - distance
    length = jnp.where(block >= 0, lengths[batch, jnp.maximum(block, 0)], 0)
    seen = key_ids < length
    if distance == 0:
        seen &= key_ids <= query_ids
    if distance == reach:
        seen &= key_ids > query_ids + (distance * rows - WINDOW)
    seen &= (query_ids + seq * rows < start) | (key_ids + block * rows >= start)
    return jnp.where(seen, 0.0, hidden)


score_factor = math.log2(math.e) * HEAD_DIM ** (-0.5)


def attend_kernel(distances, reach, lengths, boundary, queries, *refs):
    count = len(distances)
    windows, (out, tops, totals, bias) = refs[:count], refs[count:]
    rows = queries.shape[2]
    half_heads = queries.shape[1] // HEAD_DIM
    groups = windows[0].shape[2] // HEAD_DIM
    for slot, distance in enumerate(distances):
        bias[slot] = score_bias(distance, reach, rows, lengths, boundary)
    for head in range(2 * half_heads):
        half, place, side, cut = head_cuts(head, half_heads, groups)
        scores = [
            jnp.dot(
                window[side, :, cut], queries[half, place, :], preferred_element_type=jnp.float32
            )
            + bias[slot]
            for slot, window in enumerate(windows)
        ]
        top = functools.reduce(jnp.maximum, scores)
        top = jnp.max(top, axis=0, keepdims=True)
        mixed = None
        total = None
        for score, window in zip(scores, windows):
            term = jnp.exp2((score - top) * score_factor)
            total = term if total is None else total + term
            product = jnp.dot(
                window[2 + side, cut, :],
                term.astype(jnp.bfloat16),
                preferred_element_type=jnp.float32,
            )
            mixed = product if mixed is None else mixed + product
        out[half, place, :] = mixed
        tops[pl.ds(head, 1), :] = top
        totals[pl.ds(head, 1), :] = jnp.sum(total, axis=0, keepdims=True)


def attend(lengths, boundary, queries, windows, distances, reach):
    rows = queries.shape[2]
    heads = 2 * queries.shape[1] // HEAD_DIM
    span = rows * len(windows)
    return call(
        functools.partial(attend_kernel, distances, reach),
        (
            jax.ShapeDtypeStruct(queries.shape, jnp.float32),
            jax.ShapeDtypeStruct((heads, rows), jnp.float32),
            jax.ShapeDtypeStruct((heads, rows), jnp.float32),
        ),
        [smem_spec()] * 2 + [vmem_spec()] * (1 + len(windows)),
        [pltpu.VMEM((len(windows), rows, rows), jnp.float32)],
        4 * heads * rows * span * HEAD_DIM,
        2 * sum(w.size for w in windows) + 6 * queries.size,
        "attend",
        heads * rows * span,
    )(lengths, boundary, queries, *windows)


def out_kernel(
    count, distance, reach, lengths, boundary, queries, window, sums, tops, totals, state, *refs
):
    pieces, (leave, stay, mixed, chunks) = refs[: 2 * count], refs[2 * count :]
    core = lax.axis_index("segment")
    half = lax.axis_index("tp")
    seq = lax.axis_index("seq")
    place = ring_position(seq, count)
    rows = queries.shape[2]
    half_heads = queries.shape[1] // HEAD_DIM
    groups = window.shape[2] // HEAD_DIM
    bias = score_bias(distance, reach, rows, lengths, boundary)
    kept = lax.broadcasted_iota(jnp.int32, (1, rows), 1) < lengths[core, seq]
    for head in range(2 * half_heads):
        side_half, spot, side, cut = head_cuts(head, half_heads, groups)
        score = bias + jnp.dot(
            window[side, :, cut], queries[side_half, spot, :], preferred_element_type=jnp.float32
        )
        before = tops[pl.ds(head, 1), :]
        top = jnp.maximum(before, jnp.max(score, axis=0, keepdims=True))
        fade = jnp.exp2((before - top) * score_factor)
        term = jnp.exp2((score - top) * score_factor)
        total = totals[pl.ds(head, 1), :] * fade + jnp.sum(term, axis=0, keepdims=True)
        product = jnp.dot(
            window[2 + side, cut, :], term.astype(jnp.bfloat16), preferred_element_type=jnp.float32
        )
        result = (sums[side_half, spot, :] * fade + product) / total
        mixed[side_half, spot, :] = jnp.where(kept, result, 0.0).astype(jnp.bfloat16)
    for step in range(count):
        far = pieces[step].shape[0] - 1
        result = jnp.dot(pieces[step][far], mixed[core], preferred_element_type=jnp.float32)
        result += jnp.dot(
            pieces[count + step][far], mixed[1 - core], preferred_element_type=jnp.float32
        )
        chunks[ring_member(place - step, count)] = result
    parts = count // 2
    depth = chunks.shape[1]
    for part in range(parts):
        cut = slice(part * depth, (part + 1) * depth)
        leave[cut, :] = chunks[(1 - half) * parts + part].astype(jnp.bfloat16)
        stay[cut, :] = state[cut, :].astype(jnp.float32) + chunks[half * parts + part]


def out_project(lengths, boundary, queries, window, distance, reach, partial, state, own, came):
    count = len(own)
    columns, rows = queries.shape[1:]
    depth = own[0].shape[1]
    return call(
        functools.partial(out_kernel, count, distance, reach),
        (
            jax.ShapeDtypeStruct(state.shape, jnp.bfloat16),
            jax.ShapeDtypeStruct(state.shape, jnp.float32),
        ),
        [smem_spec()] * 2 + [vmem_spec()] * (6 + 2 * count),
        [
            pltpu.VMEM(queries.shape, jnp.bfloat16),
            pltpu.VMEM((count, depth, rows), jnp.float32),
        ],
        4 * count * rows * depth * columns + 8 * rows * rows * columns,
        4 * count * depth * columns + 8 * state.size,
        "out_project",
    )(lengths, boundary, queries, window, *partial, state, *own, *came)


def closed(*values):
    return lax.optimization_barrier(values)


class Ring:
    def __init__(self, shard, count):
        order = ring_order(count)
        self.onward = [(order[i], order[(i + 1) % count]) for i in range(count)]
        self.back = [(b, a) for a, b in self.onward]
        self.count = count
        self.forward = [shard]
        self.backward = [shard]
        self.far = None

    def step(self):
        if len(self.forward) < self.count // 2:
            self.forward.append(lax.ppermute(self.forward[-1], "seq", self.onward))
            self.backward.append(lax.ppermute(self.backward[-1], "seq", self.back))
        elif self.far is None:
            self.far = (
                lax.ppermute(self.forward[-1][:1], "seq", self.onward),
                lax.ppermute(self.backward[-1][1:], "seq", self.back),
            )

    def close(self, *values):
        if self.far is None:
            self.forward[-1], self.backward[-1], *rest = closed(
                self.forward[-1], self.backward[-1], *values
            )
        else:
            far_query, far_out, *rest = closed(*self.far, *values)
            self.far = (far_query, far_out)
        return rest

    def pieces(self):
        while self.far is None:
            self.step()
        far_query, far_out = self.far
        before, behind = self.forward, self.backward[:0:-1]
        return (before + [far_query] + behind, before + [far_out] + behind)


def per_device(
    inputs, lengths, boundary, attn_gain, query_weight, key_weight, value_weight, out_weight
):
    core = lax.axis_index("segment")
    seq_index = lax.axis_index("seq")
    count = lax.axis_size("seq")
    block_len = inputs.shape[1]
    first_core = core == 0

    def across_chip(value):
        return lax.ppermute(value, "segment", SWAP)

    def across_tp(value):
        return lax.ppermute(value, "tp", SWAP)

    def both_cores(pieces):
        own_query, own_out = pieces
        middle = count // 2
        came = [across_chip(piece) for piece in own_query]
        came_out = came[:middle] + [across_chip(own_out[middle])] + came[middle + 1 :]
        return own_query, came, own_out, came_out

    state = lax.dynamic_index_in_dim(jnp.swapaxes(inputs, 1, 2), core, 0, keepdims=False)
    state_other = across_tp(state)

    columns = query_weight.shape[2] // 2
    both = jnp.stack([query_weight[0], out_weight[0].T])
    mine = lax.dynamic_slice_in_dim(both, core * columns, columns, 2)
    given = lax.dynamic_slice_in_dim(both, (1 - core) * columns, columns, 2)
    came = across_chip(given)
    came, key_shard, value_shard, gain_shard = closed(
        came, key_weight[0], value_weight[0], attn_gain
    )
    shards = [jnp.where(first_core, mine, came), jnp.where(first_core, came, mine)]
    key_came, value_came = across_chip(key_shard), across_chip(value_shard)
    key_value_weights = [
        (jnp.where(first_core, key_shard, key_came), jnp.where(first_core, value_shard, value_came)),
        (jnp.where(first_core, key_came, key_shard), jnp.where(first_core, value_came, value_shard)),
    ]
    gain_came = across_chip(gain_shard)
    gains = [
        jnp.where(first_core, attn_gain, gain_came).reshape(2, -1),
        jnp.where(first_core, gain_came, attn_gain).reshape(2, -1),
    ]

    half_dim = HEAD_DIM // 2
    inverse = jnp.exp(
        -math.log(10000.0) * jnp.arange(half_dim, dtype=jnp.float32) * (2.0 / HEAD_DIM)
    )
    slots = seq_index * block_len + jnp.arange(block_len, dtype=jnp.int32)
    angles = slots.astype(jnp.float32)[:, None] * inverse[None, :]
    cosine, sine = jnp.cos(angles), jnp.sin(angles)
    tables = jnp.stack(
        [
            jnp.concatenate([cosine, cosine], axis=1),
            jnp.concatenate([-sine, sine], axis=1),
        ]
    )

    up = [(i, (i + 2) % count) for i in range(count)]
    beside = [(i, i ^ 1) for i in range(count)]
    even = seq_index % 2 == 0
    reach = max(1, WINDOW // block_len)

    def shifted(value):
        return lax.ppermute(value, "seq", up)

    def swapped(near, far):
        return lax.ppermute(jnp.where(even, near, far), "seq", beside)

    ring = Ring(shards[0], count)
    ring.step()
    states = []
    for layer in range(LAYERS):
        ring.step()
        kv_rows = key_value(
            state, state_other, gains[layer], tables, key_value_weights[layer]
        )
        evens, odds = [kv_rows], []
        for _ in range(reach // 2):
            evens.append(shifted(evens[-1]))
            if len(evens) > 2:
                odds.append(swapped(evens[-3], evens[-2]))
                evens[-1], odds[-1] = ring.close(evens[-1], odds[-1])
            else:
                (evens[-1],) = ring.close(evens[-1])
            ring.step()
        odds.append(swapped(evens[-2], evens[-1]))
        query_own, query_came, out_own, out_came = both_cores(ring.pieces())
        queries = query(state, state_other, gains[layer], tables, query_own, query_came)
        late = odds.pop()
        blocks = {2 * place: block for place, block in enumerate(evens)}
        blocks.update({2 * place + 1: block for place, block in enumerate(odds)})
        partial = attend(
            lengths, boundary, queries, list(blocks.values()), tuple(blocks), reach
        )
        if layer + 1 < LAYERS:
            late, shard, *partial = closed(late, shards[layer + 1], *partial)
            ring = Ring(shard, count)
            ring.step()
        leave, stay = out_project(
            lengths, boundary, queries, late, reach - 1, reach, partial, state, out_own, out_came
        )
        arrived = across_tp(leave)
        if layer + 1 < LAYERS:
            arrived, *key_value_weights[layer + 1] = ring.close(
                arrived, *key_value_weights[layer + 1]
            )
            ring.step()
        state = (stay + arrived.astype(jnp.float32)).astype(jnp.bfloat16)
        states.append(state)
        if layer + 1 < LAYERS:
            state_other = across_tp(state)
            (state_other,) = ring.close(state_other)

    first_came = lax.ppermute(states[0], "segment", [(1, 0)])
    last_came = lax.ppermute(states[1], "segment", [(0, 1)])
    both = jnp.stack(
        [
            jnp.where(first_core, states[0], last_came),
            jnp.where(first_core, first_came, states[1]),
        ]
    )
    return jnp.swapaxes(both, 1, 2)[None]


def solution(mesh):
    return jax.shard_map(
        per_device,
        mesh=mesh,
        in_specs=(
            P(None, "seq", "tp"),
            P(),
            P(),
            P("segment", None),
            P("segment", "seq", "tp"),
            P("segment", None, "tp"),
            P("segment", None, "tp"),
            P("segment", "tp", "seq"),
        ),
        out_specs=P("segment", None, "seq", "tp"),
        check_vma=False,
    )
```

```python
import functools
import math

import jax
import jax.numpy as jnp
from jax import lax
from jax.experimental import pallas as pl
from jax.experimental.pallas import tpu as pltpu
from jax.sharding import PartitionSpec as P

HEADS = 16
KV = 8
HEAD_DIM = 128
WINDOW = 1024
GROUP = HEADS // KV
LAYERS = 2

norm_epsilon = 1e-06
hidden = -1e30
VMEM_LIMIT = 16 * 1024 * 1024

SWAP = ((0, 1), (1, 0))


def ring_order(count):
    return list(range(0, count, 2)) + list(range(count - 1, 0, -2))


def ring_position(index, count):
    return jnp.where(index % 2 == 0, index // 2, count - 1 - index // 2)


def ring_member(position, count):
    position = lax.rem(position + 2 * count, count)
    return jnp.where(position < count // 2, 2 * position, 2 * (count - 1 - position) + 1)


def hbm_spec():
    return pl.BlockSpec(memory_space=pltpu.HBM)


def vmem_spec():
    return pl.BlockSpec(memory_space=pltpu.VMEM)


def smem_spec():
    return pl.BlockSpec(memory_space=pltpu.SMEM)


def call(kernel, out_shape, in_specs, scratch, flops, moved, name, exps=0):
    outs = jax.tree.map(lambda _: vmem_spec(), out_shape)
    return pl.pallas_call(
        kernel,
        out_shape=out_shape,
        in_specs=in_specs,
        out_specs=outs,
        scratch_shapes=scratch,
        compiler_params=pltpu.CompilerParams(vmem_limit_bytes=VMEM_LIMIT),
        cost_estimate=pl.CostEstimate(flops=flops, bytes_accessed=moved, transcendentals=exps),
        name=name,
    )


def turned(heads, cosine, sine):
    return heads * cosine + pltpu.roll(heads, HEAD_DIM // 2, 1) * sine


def norm_rows(own, other, gain, half):
    width, rows = own.shape
    total = jnp.zeros((1, rows), jnp.float32)
    for source in (own, other):
        wide = source[...].astype(jnp.float32)
        total += jnp.sum(wide * wide, axis=0, keepdims=True)
    scale = lax.rsqrt(total / (2 * width) + norm_epsilon).T
    return [
        (source[...].T.astype(jnp.float32) * scale * gain[pl.ds(which, 1), :]).astype(
            jnp.bfloat16
        )
        for source, which in ((own, half), (other, 1 - half))
    ]


def key_value_kernel(own, other, gain, tables, key, value, kv_out, normed, angles, sem):
    half = lax.axis_index("tp")
    width = own.shape[0]
    step = key.shape[1] // 2
    table_copy = pltpu.make_async_copy(tables, angles, sem)
    table_copy.start()
    normed[0], normed[1] = norm_rows(own, other, gain, half)
    table_copy.wait()
    for index in range(4):
        weight = (key, value)[index // 2]
        cut = slice(index % 2 * step, (index % 2 + 1) * step)
        result = jnp.dot(
            normed[0],
            weight[pl.ds(pl.multiple_of(half * width, 16), width), cut],
            preferred_element_type=jnp.float32,
        )
        result += jnp.dot(
            normed[1],
            weight[pl.ds(pl.multiple_of((1 - half) * width, 16), width), cut],
            preferred_element_type=jnp.float32,
        )
        if index < 2:
            for head in range(step // HEAD_DIM):
                cut = slice(head * HEAD_DIM, (head + 1) * HEAD_DIM)
                kv_out[index, :, cut] = turned(result[:, cut], angles[0], angles[1]).astype(
                    jnp.bfloat16
                )
        else:
            kv_out[index] = result.astype(jnp.bfloat16).T


def key_value(own, other, gain, tables, weights):
    width, rows = own.shape
    depth, columns = weights[0].shape
    step = columns // 2
    return call(
        key_value_kernel,
        jax.ShapeDtypeStruct((4, rows, step), jnp.bfloat16),
        [vmem_spec()] * 3 + [hbm_spec()] + [vmem_spec()] * 2,
        [
            pltpu.VMEM((2, rows, width), jnp.bfloat16),
            pltpu.VMEM(tables.shape, jnp.float32),
            pltpu.SemaphoreType.DMA(()),
        ],
        4 * rows * depth * columns,
        4 * depth * columns + 4 * rows * depth,
        "key_value",
    )(own, other, gain, tables, *weights)


def query_kernel(count, own, other, gain, tables, *refs):
    pieces, (out, normed, angles, sem) = refs[: 2 * count], refs[2 * count :]
    table_copy = pltpu.make_async_copy(tables, angles, sem)
    table_copy.start()
    core = lax.axis_index("segment")
    half = lax.axis_index("tp")
    place = ring_position(lax.axis_index("seq"), count)
    chunks, depth = count // 2, normed.shape[2]
    for rows, which in zip(norm_rows(own, other, gain, half), (half, 1 - half)):
        for part in range(chunks):
            normed[which * chunks + part] = rows[:, part * depth : (part + 1) * depth]
    table_copy.wait()
    for side in range(2):
        total = None
        for step in range(count):
            term = jnp.dot(
                normed[ring_member(place - step, count)],
                pieces[side * count + step][0],
                preferred_element_type=jnp.float32,
            )
            total = term if total is None else total + term
        target = core if side == 0 else 1 - core
        for head in range(total.shape[1] // HEAD_DIM):
            cut = slice(head * HEAD_DIM, (head + 1) * HEAD_DIM)
            rows = turned(total[:, cut], angles[0], angles[1]).astype(jnp.bfloat16)
            out[target, cut, :] = rows.T


def query(state, other, gain, tables, own, came):
    count = len(own)
    width, rows = state.shape
    depth, columns = own[0].shape[1:]
    return call(
        functools.partial(query_kernel, count),
        jax.ShapeDtypeStruct((2, columns, rows), jnp.bfloat16),
        [vmem_spec()] * 3 + [hbm_spec()] + [vmem_spec()] * (2 * count),
        [
            pltpu.VMEM((count, rows, depth), jnp.bfloat16),
            pltpu.VMEM(tables.shape, jnp.float32),
            pltpu.SemaphoreType.DMA(()),
        ],
        4 * count * rows * depth * columns,
        4 * count * depth * columns + 2 * count * rows * depth,
        "query",
    )(state, other, gain, tables, *own, *came)


def head_cuts(head, half_heads, groups):
    group = head // GROUP
    side, within = group // groups, group % groups
    cut = slice(within * HEAD_DIM, (within + 1) * HEAD_DIM)
    half, place = head // half_heads, head % half_heads
    return half, slice(place * HEAD_DIM, (place + 1) * HEAD_DIM), side, cut


def score_bias(distance, reach, rows, lengths, boundary):
    batch = lax.axis_index("segment")
    seq = lax.axis_index("seq")
    key_ids = lax.broadcasted_iota(jnp.int32, (rows, rows), 0)
    query_ids = lax.broadcasted_iota(jnp.int32, (rows, rows), 1)
    start = boundary[batch]
    block = seq - distance
    length = jnp.where(block >= 0, lengths[batch, jnp.maximum(block, 0)], 0)
    seen = key_ids < length
    if distance == 0:
        seen &= key_ids <= query_ids
    if distance == reach:
        seen &= key_ids > query_ids + (distance * rows - WINDOW)
    seen &= (query_ids + seq * rows < start) | (key_ids + block * rows >= start)
    return jnp.where(seen, 0.0, hidden)


score_factor = math.log2(math.e) * HEAD_DIM ** (-0.5)


def attend_kernel(distances, reach, lengths, boundary, queries, *refs):
    count = len(distances)
    windows, (out, tops, totals, bias) = refs[:count], refs[count:]
    rows = queries.shape[2]
    half_heads = queries.shape[1] // HEAD_DIM
    groups = windows[0].shape[2] // HEAD_DIM
    for slot, distance in enumerate(distances):
        bias[slot] = score_bias(distance, reach, rows, lengths, boundary)
    for head in range(2 * half_heads):
        half, place, side, cut = head_cuts(head, half_heads, groups)
        scores = [
            jnp.dot(
                window[side, :, cut], queries[half, place, :], preferred_element_type=jnp.float32
            )
            + bias[slot]
            for slot, window in enumerate(windows)
        ]
        top = functools.reduce(jnp.maximum, scores)
        top = jnp.max(top, axis=0, keepdims=True)
        mixed = None
        total = None
        for score, window in zip(scores, windows):
            term = jnp.exp2((score - top) * score_factor)
            total = term if total is None else total + term
            product = jnp.dot(
                window[2 + side, cut, :],
                term.astype(jnp.bfloat16),
                preferred_element_type=jnp.float32,
            )
            mixed = product if mixed is None else mixed + product
        out[half, place, :] = mixed
        tops[pl.ds(head, 1), :] = top
        totals[pl.ds(head, 1), :] = jnp.sum(total, axis=0, keepdims=True)


def attend(lengths, boundary, queries, windows, distances, reach):
    rows = queries.shape[2]
    heads = 2 * queries.shape[1] // HEAD_DIM
    span = rows * len(windows)
    return call(
        functools.partial(attend_kernel, distances, reach),
        (
            jax.ShapeDtypeStruct(queries.shape, jnp.float32),
            jax.ShapeDtypeStruct((heads, rows), jnp.float32),
            jax.ShapeDtypeStruct((heads, rows), jnp.float32),
        ),
        [smem_spec()] * 2 + [vmem_spec()] * (1 + len(windows)),
        [pltpu.VMEM((len(windows), rows, rows), jnp.float32)],
        4 * heads * rows * span * HEAD_DIM,
        2 * sum(w.size for w in windows) + 6 * queries.size,
        "attend",
        heads * rows * span,
    )(lengths, boundary, queries, *windows)


def out_kernel(
    count, distance, reach, lengths, boundary, queries, window, sums, tops, totals, state, *refs
):
    pieces, (leave, stay, mixed, chunks) = refs[: 2 * count], refs[2 * count :]
    core = lax.axis_index("segment")
    half = lax.axis_index("tp")
    seq = lax.axis_index("seq")
    place = ring_position(seq, count)
    rows = queries.shape[2]
    half_heads = queries.shape[1] // HEAD_DIM
    groups = window.shape[2] // HEAD_DIM
    bias = score_bias(distance, reach, rows, lengths, boundary)
    kept = lax.broadcasted_iota(jnp.int32, (1, rows), 1) < lengths[core, seq]
    for head in range(2 * half_heads):
        side_half, spot, side, cut = head_cuts(head, half_heads, groups)
        score = bias + jnp.dot(
            window[side, :, cut], queries[side_half, spot, :], preferred_element_type=jnp.float32
        )
        before = tops[pl.ds(head, 1), :]
        top = jnp.maximum(before, jnp.max(score, axis=0, keepdims=True))
        fade = jnp.exp2((before - top) * score_factor)
        term = jnp.exp2((score - top) * score_factor)
        total = totals[pl.ds(head, 1), :] * fade + jnp.sum(term, axis=0, keepdims=True)
        product = jnp.dot(
            window[2 + side, cut, :], term.astype(jnp.bfloat16), preferred_element_type=jnp.float32
        )
        result = (sums[side_half, spot, :] * fade + product) / total
        mixed[side_half, spot, :] = jnp.where(kept, result, 0.0).astype(jnp.bfloat16)
    for step in range(count):
        far = pieces[step].shape[0] - 1
        result = jnp.dot(pieces[step][far], mixed[core], preferred_element_type=jnp.float32)
        result += jnp.dot(
            pieces[count + step][far], mixed[1 - core], preferred_element_type=jnp.float32
        )
        chunks[ring_member(place - step, count)] = result
    parts = count // 2
    depth = chunks.shape[1]
    for part in range(parts):
        cut = slice(part * depth, (part + 1) * depth)
        leave[cut, :] = chunks[(1 - half) * parts + part].astype(jnp.bfloat16)
        stay[cut, :] = state[cut, :].astype(jnp.float32) + chunks[half * parts + part]


def out_project(lengths, boundary, queries, window, distance, reach, partial, state, own, came):
    count = len(own)
    columns, rows = queries.shape[1:]
    depth = own[0].shape[1]
    return call(
        functools.partial(out_kernel, count, distance, reach),
        (
            jax.ShapeDtypeStruct(state.shape, jnp.bfloat16),
            jax.ShapeDtypeStruct(state.shape, jnp.float32),
        ),
        [smem_spec()] * 2 + [vmem_spec()] * (6 + 2 * count),
        [
            pltpu.VMEM(queries.shape, jnp.bfloat16),
            pltpu.VMEM((count, depth, rows), jnp.float32),
        ],
        4 * count * rows * depth * columns + 8 * rows * rows * columns,
        4 * count * depth * columns + 8 * state.size,
        "out_project",
    )(lengths, boundary, queries, window, *partial, state, *own, *came)


def closed(*values):
    return lax.optimization_barrier(values)


class Ring:
    def __init__(self, shard, count):
        order = ring_order(count)
        self.onward = [(order[i], order[(i + 1) % count]) for i in range(count)]
        self.back = [(b, a) for a, b in self.onward]
        self.count = count
        self.forward = [shard]
        self.backward = [shard]
        self.far = None

    def step(self):
        if len(self.forward) < self.count // 2:
            self.forward.append(lax.ppermute(self.forward[-1], "seq", self.onward))
            self.backward.append(lax.ppermute(self.backward[-1], "seq", self.back))
        elif self.far is None:
            self.far = (
                lax.ppermute(self.forward[-1][:1], "seq", self.onward),
                lax.ppermute(self.backward[-1][1:], "seq", self.back),
            )

    def close(self, *values):
        if self.far is None:
            self.forward[-1], self.backward[-1], *rest = closed(
                self.forward[-1], self.backward[-1], *values
            )
        else:
            far_query, far_out, *rest = closed(*self.far, *values)
            self.far = (far_query, far_out)
        return rest

    def pieces(self):
        while self.far is None:
            self.step()
        far_query, far_out = self.far
        before, behind = self.forward, self.backward[:0:-1]
        return (before + [far_query] + behind, before + [far_out] + behind)


def per_device(
    inputs, lengths, boundary, attn_gain, query_weight, key_weight, value_weight, out_weight
):
    core = lax.axis_index("segment")
    seq_index = lax.axis_index("seq")
    count = lax.axis_size("seq")
    block_len = inputs.shape[1]
    first_core = core == 0

    def across_chip(value):
        return lax.ppermute(value, "segment", SWAP)

    def across_tp(value):
        return lax.ppermute(value, "tp", SWAP)

    def both_cores(pieces):
        own_query, own_out = pieces
        middle = count // 2
        came = [across_chip(piece) for piece in own_query]
        came_out = came[:middle] + [across_chip(own_out[middle])] + came[middle + 1 :]
        return own_query, came, own_out, came_out

    state = lax.dynamic_index_in_dim(jnp.swapaxes(inputs, 1, 2), core, 0, keepdims=False)
    state_other = across_tp(state)

    columns = query_weight.shape[2] // 2
    both = jnp.stack([query_weight[0], out_weight[0].T])
    mine = lax.dynamic_slice_in_dim(both, core * columns, columns, 2)
    given = lax.dynamic_slice_in_dim(both, (1 - core) * columns, columns, 2)
    came = across_chip(given)
    came, key_shard, value_shard, gain_shard = closed(
        came, key_weight[0], value_weight[0], attn_gain
    )
    shards = [jnp.where(first_core, mine, came), jnp.where(first_core, came, mine)]
    key_came, value_came = across_chip(key_shard), across_chip(value_shard)
    key_value_weights = [
        (jnp.where(first_core, key_shard, key_came), jnp.where(first_core, value_shard, value_came)),
        (jnp.where(first_core, key_came, key_shard), jnp.where(first_core, value_came, value_shard)),
    ]
    gain_came = across_chip(gain_shard)
    gains = [
        jnp.where(first_core, attn_gain, gain_came).reshape(2, -1),
        jnp.where(first_core, gain_came, attn_gain).reshape(2, -1),
    ]

    half_dim = HEAD_DIM // 2
    inverse = jnp.exp(
        -math.log(10000.0) * jnp.arange(half_dim, dtype=jnp.float32) * (2.0 / HEAD_DIM)
    )
    slots = seq_index * block_len + jnp.arange(block_len, dtype=jnp.int32)
    angles = slots.astype(jnp.float32)[:, None] * inverse[None, :]
    cosine, sine = jnp.cos(angles), jnp.sin(angles)
    tables = jnp.stack(
        [
            jnp.concatenate([cosine, cosine], axis=1),
            jnp.concatenate([-sine, sine], axis=1),
        ]
    )

    up = [(i, (i + 2) % count) for i in range(count)]
    beside = [(i, i ^ 1) for i in range(count)]
    even = seq_index % 2 == 0
    reach = max(1, WINDOW // block_len)

    def shifted(value):
        return lax.ppermute(value, "seq", up)

    def swapped(near, far):
        return lax.ppermute(jnp.where(even, near, far), "seq", beside)

    ring = Ring(shards[0], count)
    ring.step()
    states = []
    for layer in range(LAYERS):
        ring.step()
        kv_rows = key_value(
            state, state_other, gains[layer], tables, key_value_weights[layer]
        )
        evens, odds = [kv_rows], []
        for _ in range(reach // 2):
            evens.append(shifted(evens[-1]))
            if len(evens) > 2:
                odds.append(swapped(evens[-3], evens[-2]))
                evens[-1], odds[-1] = ring.close(evens[-1], odds[-1])
            else:
                if layer:
                    evens[-1], first_came = ring.close(evens[-1], first_came)
                else:
                    (evens[-1],) = ring.close(evens[-1])
            ring.step()
        odds.append(swapped(evens[-2], evens[-1]))
        query_own, query_came, out_own, out_came = both_cores(ring.pieces())
        queries = query(state, state_other, gains[layer], tables, query_own, query_came)
        late = odds.pop()
        blocks = {2 * place: block for place, block in enumerate(evens)}
        blocks.update({2 * place + 1: block for place, block in enumerate(odds)})
        partial = attend(
            lengths, boundary, queries, list(blocks.values()), tuple(blocks), reach
        )
        if layer + 1 < LAYERS:
            late, shard, *partial = closed(late, shards[layer + 1], *partial)
            ring = Ring(shard, count)
            ring.step()
        leave, stay = out_project(
            lengths, boundary, queries, late, reach - 1, reach, partial, state, out_own, out_came
        )
        if layer + 1 < LAYERS:
            arrived = across_tp(leave)
            arrived, *key_value_weights[layer + 1] = ring.close(
                arrived, *key_value_weights[layer + 1]
            )
            ring.step()
            state = (stay + arrived.astype(jnp.float32)).astype(jnp.bfloat16)
            states.append(state)
            first_came = lax.ppermute(state, "segment", [(1, 0)])
            state_other = across_tp(state)
            (state_other,) = ring.close(state_other)

    pairs = [[(2 * source + half, 3 - half) for half in range(2)] for source in range(2)]
    arrived = [lax.ppermute(leave, ("segment", "tp"), pair) for pair in pairs]
    stay_came = lax.ppermute(stay, "segment", [(0, 1)])
    both = jnp.stack(
        [
            jnp.where(
                first_core,
                states[0],
                (stay_came + arrived[0].astype(jnp.float32)).astype(jnp.bfloat16),
            ),
            jnp.where(
                first_core,
                first_came,
                (stay + arrived[1].astype(jnp.float32)).astype(jnp.bfloat16),
            ),
        ]
    )
    return jnp.swapaxes(both, 1, 2)[None]


def solution(mesh):
    return jax.shard_map(
        per_device,
        mesh=mesh,
        in_specs=(
            P(None, "seq", "tp"),
            P(),
            P(),
            P("segment", None),
            P("segment", "seq", "tp"),
            P("segment", None, "tp"),
            P("segment", None, "tp"),
            P("segment", "tp", "seq"),
        ),
        out_specs=P("segment", None, "seq", "tp"),
        check_vma=False,
    )
```

```python
import functools
import math

import jax
import jax.numpy as jnp
from jax import lax
from jax.experimental import pallas as pl
from jax.experimental.pallas import tpu as pltpu
from jax.sharding import PartitionSpec as P

HEADS = 16
KV = 8
HEAD_DIM = 128
WINDOW = 1024
GROUP = HEADS // KV
LAYERS = 2

norm_epsilon = 1e-06
hidden = -1e30
VMEM_LIMIT = 16 * 1024 * 1024

COST = 0

SWAP = ((0, 1), (1, 0))


def ring_order(count):
    return list(range(0, count, 2)) + list(range(count - 1, 0, -2))


def ring_position(index, count):
    return jnp.where(index % 2 == 0, index // 2, count - 1 - index // 2)


def ring_member(position, count):
    position = lax.rem(position + 2 * count, count)
    return jnp.where(position < count // 2, 2 * position, 2 * (count - 1 - position) + 1)


def hbm_spec():
    return pl.BlockSpec(memory_space=pltpu.HBM)


def vmem_spec():
    return pl.BlockSpec(memory_space=pltpu.VMEM)


def smem_spec():
    return pl.BlockSpec(memory_space=pltpu.SMEM)


def call(kernel, out_shape, in_specs, scratch, flops, moved, name, exps=0):
    outs = jax.tree.map(lambda _: vmem_spec(), out_shape)
    return pl.pallas_call(
        kernel,
        out_shape=out_shape,
        in_specs=in_specs,
        out_specs=outs,
        scratch_shapes=scratch,
        compiler_params=pltpu.CompilerParams(vmem_limit_bytes=VMEM_LIMIT),
        cost_estimate=pl.CostEstimate(
            flops=COST * flops, bytes_accessed=COST * moved, transcendentals=COST * exps
        ),
        name=name,
    )


def turned(heads, cosine, sine):
    return heads * cosine + pltpu.roll(heads, HEAD_DIM // 2, 1) * sine


def norm_rows(own, other, gain, half):
    width, rows = own.shape
    total = jnp.zeros((1, rows), jnp.float32)
    for source in (own, other):
        wide = source[...].astype(jnp.float32)
        total += jnp.sum(wide * wide, axis=0, keepdims=True)
    scale = lax.rsqrt(total / (2 * width) + norm_epsilon).T
    return [
        (source[...].T.astype(jnp.float32) * scale * gain[pl.ds(which, 1), :]).astype(
            jnp.bfloat16
        )
        for source, which in ((own, half), (other, 1 - half))
    ]


def key_value_kernel(own, other, gain, tables, key, value, kv_out, normed, angles, sem):
    half = lax.axis_index("tp")
    width = own.shape[0]
    step = key.shape[1] // 2
    table_copy = pltpu.make_async_copy(tables, angles, sem)
    table_copy.start()
    normed[0], normed[1] = norm_rows(own, other, gain, half)
    table_copy.wait()
    for index in range(4):
        weight = (key, value)[index // 2]
        cut = slice(index % 2 * step, (index % 2 + 1) * step)
        result = jnp.dot(
            normed[0],
            weight[pl.ds(pl.multiple_of(half * width, 16), width), cut],
            preferred_element_type=jnp.float32,
        )
        result += jnp.dot(
            normed[1],
            weight[pl.ds(pl.multiple_of((1 - half) * width, 16), width), cut],
            preferred_element_type=jnp.float32,
        )
        if index < 2:
            for head in range(step // HEAD_DIM):
                cut = slice(head * HEAD_DIM, (head + 1) * HEAD_DIM)
                kv_out[index, :, cut] = turned(result[:, cut], angles[0], angles[1]).astype(
                    jnp.bfloat16
                )
        else:
            kv_out[index] = result.astype(jnp.bfloat16).T


def key_value(own, other, gain, tables, weights):
    width, rows = own.shape
    depth, columns = weights[0].shape
    step = columns // 2
    return call(
        key_value_kernel,
        jax.ShapeDtypeStruct((4, rows, step), jnp.bfloat16),
        [vmem_spec()] * 3 + [hbm_spec()] + [vmem_spec()] * 2,
        [
            pltpu.VMEM((2, rows, width), jnp.bfloat16),
            pltpu.VMEM(tables.shape, jnp.float32),
            pltpu.SemaphoreType.DMA(()),
        ],
        4 * rows * depth * columns,
        4 * depth * columns + 4 * rows * depth,
        "key_value",
    )(own, other, gain, tables, *weights)


def query_kernel(count, own, other, gain, tables, *refs):
    pieces, (out, normed, angles, sem) = refs[: 2 * count], refs[2 * count :]
    table_copy = pltpu.make_async_copy(tables, angles, sem)
    table_copy.start()
    core = lax.axis_index("segment")
    half = lax.axis_index("tp")
    place = ring_position(lax.axis_index("seq"), count)
    chunks, depth = count // 2, normed.shape[2]
    for rows, which in zip(norm_rows(own, other, gain, half), (half, 1 - half)):
        for part in range(chunks):
            normed[which * chunks + part] = rows[:, part * depth : (part + 1) * depth]
    table_copy.wait()
    for side in range(2):
        total = None
        for step in range(count):
            term = jnp.dot(
                normed[ring_member(place - step, count)],
                pieces[side * count + step][0],
                preferred_element_type=jnp.float32,
            )
            total = term if total is None else total + term
        target = core if side == 0 else 1 - core
        for head in range(total.shape[1] // HEAD_DIM):
            cut = slice(head * HEAD_DIM, (head + 1) * HEAD_DIM)
            rows = turned(total[:, cut], angles[0], angles[1]).astype(jnp.bfloat16)
            out[target, cut, :] = rows.T


def query(state, other, gain, tables, own, came):
    count = len(own)
    width, rows = state.shape
    depth, columns = own[0].shape[1:]
    return call(
        functools.partial(query_kernel, count),
        jax.ShapeDtypeStruct((2, columns, rows), jnp.bfloat16),
        [vmem_spec()] * 3 + [hbm_spec()] + [vmem_spec()] * (2 * count),
        [
            pltpu.VMEM((count, rows, depth), jnp.bfloat16),
            pltpu.VMEM(tables.shape, jnp.float32),
            pltpu.SemaphoreType.DMA(()),
        ],
        4 * count * rows * depth * columns,
        4 * count * depth * columns + 2 * count * rows * depth,
        "query",
    )(state, other, gain, tables, *own, *came)


def head_cuts(head, half_heads, groups):
    group = head // GROUP
    side, within = group // groups, group % groups
    cut = slice(within * HEAD_DIM, (within + 1) * HEAD_DIM)
    half, place = head // half_heads, head % half_heads
    return half, slice(place * HEAD_DIM, (place + 1) * HEAD_DIM), side, cut


def score_bias(distance, reach, rows, lengths, boundary):
    batch = lax.axis_index("segment")
    seq = lax.axis_index("seq")
    key_ids = lax.broadcasted_iota(jnp.int32, (rows, rows), 0)
    query_ids = lax.broadcasted_iota(jnp.int32, (rows, rows), 1)
    start = boundary[batch]
    block = seq - distance
    length = jnp.where(block >= 0, lengths[batch, jnp.maximum(block, 0)], 0)
    seen = key_ids < length
    if distance == 0:
        seen &= key_ids <= query_ids
    if distance == reach:
        seen &= key_ids > query_ids + (distance * rows - WINDOW)
    seen &= (query_ids + seq * rows < start) | (key_ids + block * rows >= start)
    return jnp.where(seen, 0.0, hidden)


score_factor = math.log2(math.e) * HEAD_DIM ** (-0.5)


def attend_kernel(distances, reach, lengths, boundary, queries, *refs):
    count = len(distances)
    windows, (out, tops, totals, bias) = refs[:count], refs[count:]
    rows = queries.shape[2]
    half_heads = queries.shape[1] // HEAD_DIM
    groups = windows[0].shape[2] // HEAD_DIM
    for slot, distance in enumerate(distances):
        bias[slot] = score_bias(distance, reach, rows, lengths, boundary)
    for head in range(2 * half_heads):
        half, place, side, cut = head_cuts(head, half_heads, groups)
        scores = [
            jnp.dot(
                window[side, :, cut], queries[half, place, :], preferred_element_type=jnp.float32
            )
            + bias[slot]
            for slot, window in enumerate(windows)
        ]
        top = functools.reduce(jnp.maximum, scores)
        top = jnp.max(top, axis=0, keepdims=True)
        mixed = None
        total = None
        for score, window in zip(scores, windows):
            term = jnp.exp2((score - top) * score_factor)
            total = term if total is None else total + term
            product = jnp.dot(
                window[2 + side, cut, :],
                term.astype(jnp.bfloat16),
                preferred_element_type=jnp.float32,
            )
            mixed = product if mixed is None else mixed + product
        out[half, place, :] = mixed
        tops[pl.ds(head, 1), :] = top
        totals[pl.ds(head, 1), :] = jnp.sum(total, axis=0, keepdims=True)


def attend(lengths, boundary, queries, windows, distances, reach):
    rows = queries.shape[2]
    heads = 2 * queries.shape[1] // HEAD_DIM
    span = rows * len(windows)
    return call(
        functools.partial(attend_kernel, distances, reach),
        (
            jax.ShapeDtypeStruct(queries.shape, jnp.float32),
            jax.ShapeDtypeStruct((heads, rows), jnp.float32),
            jax.ShapeDtypeStruct((heads, rows), jnp.float32),
        ),
        [smem_spec()] * 2 + [vmem_spec()] * (1 + len(windows)),
        [pltpu.VMEM((len(windows), rows, rows), jnp.float32)],
        4 * heads * rows * span * HEAD_DIM,
        2 * sum(w.size for w in windows) + 6 * queries.size,
        "attend",
        heads * rows * span,
    )(lengths, boundary, queries, *windows)


def out_kernel(
    count, distance, reach, lengths, boundary, queries, window, sums, tops, totals, state, *refs
):
    pieces, (leave, stay, mixed, chunks) = refs[: 2 * count], refs[2 * count :]
    core = lax.axis_index("segment")
    half = lax.axis_index("tp")
    seq = lax.axis_index("seq")
    place = ring_position(seq, count)
    rows = queries.shape[2]
    half_heads = queries.shape[1] // HEAD_DIM
    groups = window.shape[2] // HEAD_DIM
    bias = score_bias(distance, reach, rows, lengths, boundary)
    kept = lax.broadcasted_iota(jnp.int32, (1, rows), 1) < lengths[core, seq]
    for head in range(2 * half_heads):
        side_half, spot, side, cut = head_cuts(head, half_heads, groups)
        score = bias + jnp.dot(
            window[side, :, cut], queries[side_half, spot, :], preferred_element_type=jnp.float32
        )
        before = tops[pl.ds(head, 1), :]
        top = jnp.maximum(before, jnp.max(score, axis=0, keepdims=True))
        fade = jnp.exp2((before - top) * score_factor)
        term = jnp.exp2((score - top) * score_factor)
        total = totals[pl.ds(head, 1), :] * fade + jnp.sum(term, axis=0, keepdims=True)
        product = jnp.dot(
            window[2 + side, cut, :], term.astype(jnp.bfloat16), preferred_element_type=jnp.float32
        )
        result = (sums[side_half, spot, :] * fade + product) / total
        mixed[side_half, spot, :] = jnp.where(kept, result, 0.0).astype(jnp.bfloat16)
    for step in range(count):
        far = pieces[step].shape[0] - 1
        result = jnp.dot(pieces[step][far], mixed[core], preferred_element_type=jnp.float32)
        result += jnp.dot(
            pieces[count + step][far], mixed[1 - core], preferred_element_type=jnp.float32
        )
        chunks[ring_member(place - step, count)] = result
    parts = count // 2
    depth = chunks.shape[1]
    for part in range(parts):
        cut = slice(part * depth, (part + 1) * depth)
        leave[cut, :] = chunks[(1 - half) * parts + part].astype(jnp.bfloat16)
        stay[cut, :] = state[cut, :].astype(jnp.float32) + chunks[half * parts + part]


def out_project(lengths, boundary, queries, window, distance, reach, partial, state, own, came):
    count = len(own)
    columns, rows = queries.shape[1:]
    depth = own[0].shape[1]
    return call(
        functools.partial(out_kernel, count, distance, reach),
        (
            jax.ShapeDtypeStruct(state.shape, jnp.bfloat16),
            jax.ShapeDtypeStruct(state.shape, jnp.float32),
        ),
        [smem_spec()] * 2 + [vmem_spec()] * (6 + 2 * count),
        [
            pltpu.VMEM(queries.shape, jnp.bfloat16),
            pltpu.VMEM((count, depth, rows), jnp.float32),
        ],
        4 * count * rows * depth * columns + 8 * rows * rows * columns,
        4 * count * depth * columns + 8 * state.size,
        "out_project",
    )(lengths, boundary, queries, window, *partial, state, *own, *came)


def closed(*values):
    return lax.optimization_barrier(values)


class Ring:
    def __init__(self, shard, count):
        order = ring_order(count)
        self.onward = [(order[i], order[(i + 1) % count]) for i in range(count)]
        self.back = [(b, a) for a, b in self.onward]
        self.count = count
        self.forward = [shard]
        self.backward = [shard]
        self.far = None

    def step(self):
        if len(self.forward) < self.count // 2:
            self.forward.append(lax.ppermute(self.forward[-1], "seq", self.onward))
            self.backward.append(lax.ppermute(self.backward[-1], "seq", self.back))
        elif self.far is None:
            self.far = (
                lax.ppermute(self.forward[-1][:1], "seq", self.onward),
                lax.ppermute(self.backward[-1][1:], "seq", self.back),
            )

    def close(self, *values):
        if self.far is None:
            self.forward[-1], self.backward[-1], *rest = closed(
                self.forward[-1], self.backward[-1], *values
            )
        else:
            far_query, far_out, *rest = closed(*self.far, *values)
            self.far = (far_query, far_out)
        return rest

    def pieces(self):
        while self.far is None:
            self.step()
        far_query, far_out = self.far
        before, behind = self.forward, self.backward[:0:-1]
        return (before + [far_query] + behind, before + [far_out] + behind)


def per_device(
    inputs, lengths, boundary, attn_gain, query_weight, key_weight, value_weight, out_weight
):
    core = lax.axis_index("segment")
    seq_index = lax.axis_index("seq")
    count = lax.axis_size("seq")
    block_len = inputs.shape[1]
    first_core = core == 0

    def across_chip(value):
        return lax.ppermute(value, "segment", SWAP)

    def across_tp(value):
        return lax.ppermute(value, "tp", SWAP)

    def both_cores(pieces):
        own_query, own_out = pieces
        middle = count // 2
        came = [across_chip(piece) for piece in own_query]
        came_out = came[:middle] + [across_chip(own_out[middle])] + came[middle + 1 :]
        return own_query, came, own_out, came_out

    state = lax.dynamic_index_in_dim(jnp.swapaxes(inputs, 1, 2), core, 0, keepdims=False)
    state_other = across_tp(state)

    columns = query_weight.shape[2] // 2
    both = jnp.stack([query_weight[0], out_weight[0].T])
    mine = lax.dynamic_slice_in_dim(both, core * columns, columns, 2)
    given = lax.dynamic_slice_in_dim(both, (1 - core) * columns, columns, 2)
    came = across_chip(given)
    came, key_shard, value_shard, gain_shard = closed(
        came, key_weight[0], value_weight[0], attn_gain
    )
    shards = [jnp.where(first_core, mine, came), jnp.where(first_core, came, mine)]
    key_came, value_came = across_chip(key_shard), across_chip(value_shard)
    key_value_weights = [
        (jnp.where(first_core, key_shard, key_came), jnp.where(first_core, value_shard, value_came)),
        (jnp.where(first_core, key_came, key_shard), jnp.where(first_core, value_came, value_shard)),
    ]
    gain_came = across_chip(gain_shard)
    gains = [
        jnp.where(first_core, attn_gain, gain_came).reshape(2, -1),
        jnp.where(first_core, gain_came, attn_gain).reshape(2, -1),
    ]

    half_dim = HEAD_DIM // 2
    inverse = jnp.exp(
        -math.log(10000.0) * jnp.arange(half_dim, dtype=jnp.float32) * (2.0 / HEAD_DIM)
    )
    slots = seq_index * block_len + jnp.arange(block_len, dtype=jnp.int32)
    angles = slots.astype(jnp.float32)[:, None] * inverse[None, :]
    cosine, sine = jnp.cos(angles), jnp.sin(angles)
    tables = jnp.stack(
        [
            jnp.concatenate([cosine, cosine], axis=1),
            jnp.concatenate([-sine, sine], axis=1),
        ]
    )

    up = [(i, (i + 2) % count) for i in range(count)]
    beside = [(i, i ^ 1) for i in range(count)]
    even = seq_index % 2 == 0
    reach = max(1, WINDOW // block_len)

    def shifted(value):
        return lax.ppermute(value, "seq", up)

    def swapped(near, far):
        return lax.ppermute(jnp.where(even, near, far), "seq", beside)

    ring = Ring(shards[0], count)
    ring.step()
    states = []
    for layer in range(LAYERS):
        ring.step()
        kv_rows = key_value(
            state, state_other, gains[layer], tables, key_value_weights[layer]
        )
        evens, odds = [kv_rows], []
        for _ in range(reach // 2):
            evens.append(shifted(evens[-1]))
            if len(evens) > 2:
                odds.append(swapped(evens[-3], evens[-2]))
                evens[-1], odds[-1] = ring.close(evens[-1], odds[-1])
                ring.step()
            elif layer:
                evens[-1], first_came = ring.close(evens[-1], first_came)
            else:
                (evens[-1],) = ring.close(evens[-1])
                ring.step()
        odds.append(swapped(evens[-2], evens[-1]))
        query_own, query_came, out_own, out_came = both_cores(ring.pieces())
        queries = query(state, state_other, gains[layer], tables, query_own, query_came)
        late = odds.pop()
        blocks = {2 * place: block for place, block in enumerate(evens)}
        blocks.update({2 * place + 1: block for place, block in enumerate(odds)})
        partial = attend(
            lengths, boundary, queries, list(blocks.values()), tuple(blocks), reach
        )
        if layer + 1 < LAYERS:
            late, shard, *partial = closed(late, shards[layer + 1], *partial)
            ring = Ring(shard, count)
            ring.step()
        leave, stay = out_project(
            lengths, boundary, queries, late, reach - 1, reach, partial, state, out_own, out_came
        )
        if layer + 1 < LAYERS:
            arrived = across_tp(leave)
            arrived, *key_value_weights[layer + 1] = ring.close(
                arrived, *key_value_weights[layer + 1]
            )
            ring.step()
            state = (stay + arrived.astype(jnp.float32)).astype(jnp.bfloat16)
            states.append(state)
            first_came = lax.ppermute(state, "segment", [(1, 0)])
            state_other = across_tp(state)
            (state_other,) = ring.close(state_other)

    pairs = [[(2 * source + half, 3 - half) for half in range(2)] for source in range(2)]
    arrived = [lax.ppermute(leave, ("segment", "tp"), pair) for pair in pairs]
    stay_came = lax.ppermute(stay, "segment", [(0, 1)])
    both = jnp.stack(
        [
            jnp.where(
                first_core,
                states[0],
                (stay_came + arrived[0].astype(jnp.float32)).astype(jnp.bfloat16),
            ),
            jnp.where(
                first_core,
                first_came,
                (stay + arrived[1].astype(jnp.float32)).astype(jnp.bfloat16),
            ),
        ]
    )
    return jnp.swapaxes(both, 1, 2)[None]


def solution(mesh):
    return jax.shard_map(
        per_device,
        mesh=mesh,
        in_specs=(
            P(None, "seq", "tp"),
            P(),
            P(),
            P("segment", None),
            P("segment", "seq", "tp"),
            P("segment", None, "tp"),
            P("segment", None, "tp"),
            P("segment", "tp", "seq"),
        ),
        out_specs=P("segment", None, "seq", "tp"),
        check_vma=False,
    )
```

```python
import functools
import math

import jax
import jax.numpy as jnp
from jax import lax
from jax.experimental import pallas as pl
from jax.experimental.pallas import tpu as pltpu
from jax.sharding import PartitionSpec as P

HEADS = 16
KV = 8
HEAD_DIM = 128
WINDOW = 1024
GROUP = HEADS // KV
LAYERS = 2

norm_epsilon = 1e-06
hidden = -1e30
VMEM_LIMIT = 16 * 1024 * 1024

COST = 0

SWAP = ((0, 1), (1, 0))


def ring_order(count):
    return list(range(0, count, 2)) + list(range(count - 1, 0, -2))


def ring_position(index, count):
    return jnp.where(index % 2 == 0, index // 2, count - 1 - index // 2)


def ring_member(position, count):
    position = lax.rem(position + 2 * count, count)
    return jnp.where(position < count // 2, 2 * position, 2 * (count - 1 - position) + 1)


def hbm_spec():
    return pl.BlockSpec(memory_space=pltpu.HBM)


def vmem_spec():
    return pl.BlockSpec(memory_space=pltpu.VMEM)


def smem_spec():
    return pl.BlockSpec(memory_space=pltpu.SMEM)


def call(kernel, out_shape, in_specs, scratch, flops, moved, name, exps=0):
    outs = jax.tree.map(lambda _: vmem_spec(), out_shape)
    return pl.pallas_call(
        kernel,
        out_shape=out_shape,
        in_specs=in_specs,
        out_specs=outs,
        scratch_shapes=scratch,
        compiler_params=pltpu.CompilerParams(vmem_limit_bytes=VMEM_LIMIT),
        cost_estimate=pl.CostEstimate(
            flops=COST * flops, bytes_accessed=COST * moved, transcendentals=COST * exps
        ),
        name=name,
    )


def turned(heads, cosine, sine):
    return heads * cosine + pltpu.roll(heads, HEAD_DIM // 2, 1) * sine


def norm_rows(own, other, gain, half):
    width, rows = own.shape
    total = jnp.zeros((1, rows), jnp.float32)
    for source in (own, other):
        wide = source[...].astype(jnp.float32)
        total += jnp.sum(wide * wide, axis=0, keepdims=True)
    scale = lax.rsqrt(total / (2 * width) + norm_epsilon).T
    return [
        (source[...].T.astype(jnp.float32) * scale * gain[pl.ds(which, 1), :]).astype(
            jnp.bfloat16
        )
        for source, which in ((own, half), (other, 1 - half))
    ]


def key_value_kernel(own, other, gain, tables, key, value, kv_out, normed, angles, sem):
    half = lax.axis_index("tp")
    width = own.shape[0]
    step = key.shape[1] // 2
    table_copy = pltpu.make_async_copy(tables, angles, sem)
    table_copy.start()
    normed[0], normed[1] = norm_rows(own, other, gain, half)
    table_copy.wait()
    for index in range(4):
        weight = (key, value)[index // 2]
        cut = slice(index % 2 * step, (index % 2 + 1) * step)
        result = jnp.dot(
            normed[0],
            weight[pl.ds(pl.multiple_of(half * width, 16), width), cut],
            preferred_element_type=jnp.float32,
        )
        result += jnp.dot(
            normed[1],
            weight[pl.ds(pl.multiple_of((1 - half) * width, 16), width), cut],
            preferred_element_type=jnp.float32,
        )
        if index < 2:
            for head in range(step // HEAD_DIM):
                cut = slice(head * HEAD_DIM, (head + 1) * HEAD_DIM)
                kv_out[index, :, cut] = turned(result[:, cut], angles[0], angles[1]).astype(
                    jnp.bfloat16
                )
        else:
            kv_out[index] = result.astype(jnp.bfloat16).T


def key_value(own, other, gain, tables, weights):
    width, rows = own.shape
    depth, columns = weights[0].shape
    step = columns // 2
    return call(
        key_value_kernel,
        jax.ShapeDtypeStruct((4, rows, step), jnp.bfloat16),
        [vmem_spec()] * 3 + [hbm_spec()] + [vmem_spec()] * 2,
        [
            pltpu.VMEM((2, rows, width), jnp.bfloat16),
            pltpu.VMEM(tables.shape, jnp.float32),
            pltpu.SemaphoreType.DMA(()),
        ],
        4 * rows * depth * columns,
        4 * depth * columns + 4 * rows * depth,
        "key_value",
    )(own, other, gain, tables, *weights)


def query_kernel(count, own, other, gain, tables, *refs):
    pieces, (out, normed, angles, sem) = refs[: 2 * count], refs[2 * count :]
    table_copy = pltpu.make_async_copy(tables, angles, sem)
    table_copy.start()
    core = lax.axis_index("segment")
    half = lax.axis_index("tp")
    place = ring_position(lax.axis_index("seq"), count)
    chunks, depth = count // 2, normed.shape[2]
    for rows, which in zip(norm_rows(own, other, gain, half), (half, 1 - half)):
        for part in range(chunks):
            normed[which * chunks + part] = rows[:, part * depth : (part + 1) * depth]
    table_copy.wait()
    for side in range(2):
        total = None
        for step in range(count):
            term = jnp.dot(
                normed[ring_member(place - step, count)],
                pieces[side * count + step][0],
                preferred_element_type=jnp.float32,
            )
            total = term if total is None else total + term
        target = core if side == 0 else 1 - core
        for head in range(total.shape[1] // HEAD_DIM):
            cut = slice(head * HEAD_DIM, (head + 1) * HEAD_DIM)
            rows = turned(total[:, cut], angles[0], angles[1]).astype(jnp.bfloat16)
            out[target, cut, :] = rows.T


def query(state, other, gain, tables, own, came):
    count = len(own)
    width, rows = state.shape
    depth, columns = own[0].shape[1:]
    return call(
        functools.partial(query_kernel, count),
        jax.ShapeDtypeStruct((2, columns, rows), jnp.bfloat16),
        [vmem_spec()] * 3 + [hbm_spec()] + [vmem_spec()] * (2 * count),
        [
            pltpu.VMEM((count, rows, depth), jnp.bfloat16),
            pltpu.VMEM(tables.shape, jnp.float32),
            pltpu.SemaphoreType.DMA(()),
        ],
        4 * count * rows * depth * columns,
        4 * count * depth * columns + 2 * count * rows * depth,
        "query",
    )(state, other, gain, tables, *own, *came)


def head_cuts(head, half_heads, groups):
    group = head // GROUP
    side, within = group // groups, group % groups
    cut = slice(within * HEAD_DIM, (within + 1) * HEAD_DIM)
    half, place = head // half_heads, head % half_heads
    return half, slice(place * HEAD_DIM, (place + 1) * HEAD_DIM), side, cut


def score_bias(distance, reach, rows, lengths, boundary):
    batch = lax.axis_index("segment")
    seq = lax.axis_index("seq")
    key_ids = lax.broadcasted_iota(jnp.int32, (rows, rows), 0)
    query_ids = lax.broadcasted_iota(jnp.int32, (rows, rows), 1)
    start = boundary[batch]
    block = seq - distance
    length = jnp.where(block >= 0, lengths[batch, jnp.maximum(block, 0)], 0)
    seen = key_ids < length
    if distance == 0:
        seen &= key_ids <= query_ids
    if distance == reach:
        seen &= key_ids > query_ids + (distance * rows - WINDOW)
    seen &= (query_ids + seq * rows < start) | (key_ids + block * rows >= start)
    return jnp.where(seen, 0.0, hidden)


score_factor = math.log2(math.e) * HEAD_DIM ** (-0.5)


def attend_kernel(distances, reach, lengths, boundary, queries, *refs):
    count = len(distances)
    windows, (out, tops, totals, bias) = refs[:count], refs[count:]
    rows = queries.shape[2]
    half_heads = queries.shape[1] // HEAD_DIM
    groups = windows[0].shape[2] // HEAD_DIM
    for slot, distance in enumerate(distances):
        bias[slot] = score_bias(distance, reach, rows, lengths, boundary)
    for head in range(2 * half_heads):
        half, place, side, cut = head_cuts(head, half_heads, groups)
        scores = [
            jnp.dot(
                window[side, :, cut], queries[half, place, :], preferred_element_type=jnp.float32
            )
            + bias[slot]
            for slot, window in enumerate(windows)
        ]
        top = functools.reduce(jnp.maximum, scores)
        top = jnp.max(top, axis=0, keepdims=True)
        mixed = None
        total = None
        for score, window in zip(scores, windows):
            term = jnp.exp2((score - top) * score_factor)
            total = term if total is None else total + term
            product = jnp.dot(
                window[2 + side, cut, :],
                term.astype(jnp.bfloat16),
                preferred_element_type=jnp.float32,
            )
            mixed = product if mixed is None else mixed + product
        out[half, place, :] = mixed
        tops[pl.ds(head, 1), :] = top
        totals[pl.ds(head, 1), :] = jnp.sum(total, axis=0, keepdims=True)


def attend(lengths, boundary, queries, windows, distances, reach):
    rows = queries.shape[2]
    heads = 2 * queries.shape[1] // HEAD_DIM
    span = rows * len(windows)
    return call(
        functools.partial(attend_kernel, distances, reach),
        (
            jax.ShapeDtypeStruct(queries.shape, jnp.float32),
            jax.ShapeDtypeStruct((heads, rows), jnp.float32),
            jax.ShapeDtypeStruct((heads, rows), jnp.float32),
        ),
        [smem_spec()] * 2 + [vmem_spec()] * (1 + len(windows)),
        [pltpu.VMEM((len(windows), rows, rows), jnp.float32)],
        4 * heads * rows * span * HEAD_DIM,
        2 * sum(w.size for w in windows) + 6 * queries.size,
        "attend",
        heads * rows * span,
    )(lengths, boundary, queries, *windows)


def out_kernel(
    count, distance, reach, lengths, boundary, queries, window, sums, tops, totals, state, *refs
):
    pieces, (leave, stay, mixed, chunks) = refs[: 2 * count], refs[2 * count :]
    core = lax.axis_index("segment")
    half = lax.axis_index("tp")
    seq = lax.axis_index("seq")
    place = ring_position(seq, count)
    rows = queries.shape[2]
    half_heads = queries.shape[1] // HEAD_DIM
    groups = window.shape[2] // HEAD_DIM
    bias = score_bias(distance, reach, rows, lengths, boundary)
    kept = lax.broadcasted_iota(jnp.int32, (1, rows), 1) < lengths[core, seq]
    for head in range(2 * half_heads):
        side_half, spot, side, cut = head_cuts(head, half_heads, groups)
        score = bias + jnp.dot(
            window[side, :, cut], queries[side_half, spot, :], preferred_element_type=jnp.float32
        )
        before = tops[pl.ds(head, 1), :]
        top = jnp.maximum(before, jnp.max(score, axis=0, keepdims=True))
        fade = jnp.exp2((before - top) * score_factor)
        term = jnp.exp2((score - top) * score_factor)
        total = totals[pl.ds(head, 1), :] * fade + jnp.sum(term, axis=0, keepdims=True)
        product = jnp.dot(
            window[2 + side, cut, :], term.astype(jnp.bfloat16), preferred_element_type=jnp.float32
        )
        result = (sums[side_half, spot, :] * fade + product) / total
        mixed[side_half, spot, :] = jnp.where(kept, result, 0.0).astype(jnp.bfloat16)
    for step in range(count):
        far = pieces[step].shape[0] - 1
        result = jnp.dot(pieces[step][far], mixed[core], preferred_element_type=jnp.float32)
        result += jnp.dot(
            pieces[count + step][far], mixed[1 - core], preferred_element_type=jnp.float32
        )
        chunks[ring_member(place - step, count)] = result
    parts = count // 2
    depth = chunks.shape[1]
    for part in range(parts):
        cut = slice(part * depth, (part + 1) * depth)
        leave[cut, :] = chunks[(1 - half) * parts + part].astype(jnp.bfloat16)
        stay[cut, :] = state[cut, :].astype(jnp.float32) + chunks[half * parts + part]


def out_project(lengths, boundary, queries, window, distance, reach, partial, state, own, came):
    count = len(own)
    columns, rows = queries.shape[1:]
    depth = own[0].shape[1]
    return call(
        functools.partial(out_kernel, count, distance, reach),
        (
            jax.ShapeDtypeStruct(state.shape, jnp.bfloat16),
            jax.ShapeDtypeStruct(state.shape, jnp.float32),
        ),
        [smem_spec()] * 2 + [vmem_spec()] * (6 + 2 * count),
        [
            pltpu.VMEM(queries.shape, jnp.bfloat16),
            pltpu.VMEM((count, depth, rows), jnp.float32),
        ],
        4 * count * rows * depth * columns + 8 * rows * rows * columns,
        4 * count * depth * columns + 8 * state.size,
        "out_project",
    )(lengths, boundary, queries, window, *partial, state, *own, *came)


def closed(*values):
    return lax.optimization_barrier(values)


class Ring:
    def __init__(self, shard, count):
        order = ring_order(count)
        self.onward = [(order[i], order[(i + 1) % count]) for i in range(count)]
        self.back = [(b, a) for a, b in self.onward]
        self.count = count
        self.forward = [shard]
        self.backward = [shard]
        self.far = None

    def step(self):
        if len(self.forward) < self.count // 2:
            self.forward.append(lax.ppermute(self.forward[-1], "seq", self.onward))
            self.backward.append(lax.ppermute(self.backward[-1], "seq", self.back))
        elif self.far is None:
            self.far = (
                lax.ppermute(self.forward[-1][:1], "seq", self.onward),
                lax.ppermute(self.backward[-1][1:], "seq", self.back),
            )

    def close(self, *values):
        if self.far is None:
            self.forward[-1], self.backward[-1], *rest = closed(
                self.forward[-1], self.backward[-1], *values
            )
        else:
            far_query, far_out, *rest = closed(*self.far, *values)
            self.far = (far_query, far_out)
        return rest

    def pieces(self):
        while self.far is None:
            self.step()
        far_query, far_out = self.far
        before, behind = self.forward, self.backward[:0:-1]
        return (before + [far_query] + behind, before + [far_out] + behind)


def per_device(
    inputs, lengths, boundary, attn_gain, query_weight, key_weight, value_weight, out_weight
):
    core = lax.axis_index("segment")
    seq_index = lax.axis_index("seq")
    count = lax.axis_size("seq")
    block_len = inputs.shape[1]
    first_core = core == 0

    def across_chip(value):
        return lax.ppermute(value, "segment", SWAP)

    def across_tp(value):
        return lax.ppermute(value, "tp", SWAP)

    def both_cores(pieces):
        own_query, own_out = pieces
        middle = count // 2
        came = [across_chip(piece) for piece in own_query]
        came_out = came[:middle] + [across_chip(own_out[middle])] + came[middle + 1 :]
        return own_query, came, own_out, came_out

    state = lax.dynamic_index_in_dim(jnp.swapaxes(inputs, 1, 2), core, 0, keepdims=False)
    state_other = across_tp(state)

    columns = query_weight.shape[2] // 2
    both = jnp.stack([query_weight[0], out_weight[0].T])
    mine = lax.dynamic_slice_in_dim(both, core * columns, columns, 2)
    given = lax.dynamic_slice_in_dim(both, (1 - core) * columns, columns, 2)
    came = across_chip(given)
    came, key_shard, value_shard, gain_shard = closed(
        came, key_weight[0], value_weight[0], attn_gain
    )
    shards = [jnp.where(first_core, mine, came), jnp.where(first_core, came, mine)]
    key_came, value_came = across_chip(key_shard), across_chip(value_shard)
    key_value_weights = [
        (jnp.where(first_core, key_shard, key_came), jnp.where(first_core, value_shard, value_came)),
        (jnp.where(first_core, key_came, key_shard), jnp.where(first_core, value_came, value_shard)),
    ]
    gain_came = across_chip(gain_shard)
    gains = [
        jnp.where(first_core, attn_gain, gain_came).reshape(2, -1),
        jnp.where(first_core, gain_came, attn_gain).reshape(2, -1),
    ]

    half_dim = HEAD_DIM // 2
    inverse = jnp.exp(
        -math.log(10000.0) * jnp.arange(half_dim, dtype=jnp.float32) * (2.0 / HEAD_DIM)
    )
    slots = seq_index * block_len + jnp.arange(block_len, dtype=jnp.int32)
    angles = slots.astype(jnp.float32)[:, None] * inverse[None, :]
    cosine, sine = jnp.cos(angles), jnp.sin(angles)
    tables = jnp.stack(
        [
            jnp.concatenate([cosine, cosine], axis=1),
            jnp.concatenate([-sine, sine], axis=1),
        ]
    )

    up = [(i, (i + 2) % count) for i in range(count)]
    beside = [(i, i ^ 1) for i in range(count)]
    even = seq_index % 2 == 0
    reach = max(1, WINDOW // block_len)

    def shifted(value):
        return lax.ppermute(value, "seq", up)

    def swapped(near, far):
        return lax.ppermute(jnp.where(even, near, far), "seq", beside)

    ring = Ring(shards[0], count)
    ring.step()
    key_value_weights[0] = ring.close(*key_value_weights[0])
    states = []
    for layer in range(LAYERS):
        ring.step()
        kv_rows = key_value(
            state, state_other, gains[layer], tables, key_value_weights[layer]
        )
        evens, odds = [kv_rows], []
        for _ in range(reach // 2):
            evens.append(shifted(evens[-1]))
            if len(evens) > 2:
                odds.append(swapped(evens[-3], evens[-2]))
                evens[-1], odds[-1] = ring.close(evens[-1], odds[-1])
                ring.step()
            elif layer:
                evens[-1], first_came = ring.close(evens[-1], first_came)
            else:
                (evens[-1],) = ring.close(evens[-1])
                ring.step()
        odds.append(swapped(evens[-2], evens[-1]))
        query_own, query_came, out_own, out_came = both_cores(ring.pieces())
        queries = query(state, state_other, gains[layer], tables, query_own, query_came)
        late = odds.pop()
        blocks = {2 * place: block for place, block in enumerate(evens)}
        blocks.update({2 * place + 1: block for place, block in enumerate(odds)})
        partial = attend(
            lengths, boundary, queries, list(blocks.values()), tuple(blocks), reach
        )
        if layer + 1 < LAYERS:
            late, shard, *partial = closed(late, shards[layer + 1], *partial)
            ring = Ring(shard, count)
            ring.step()
        leave, stay = out_project(
            lengths, boundary, queries, late, reach - 1, reach, partial, state, out_own, out_came
        )
        if layer + 1 < LAYERS:
            arrived = across_tp(leave)
            arrived, *key_value_weights[layer + 1] = ring.close(
                arrived, *key_value_weights[layer + 1]
            )
            ring.step()
            state = (stay + arrived.astype(jnp.float32)).astype(jnp.bfloat16)
            states.append(state)
            first_came = lax.ppermute(state, "segment", [(1, 0)])
            state_other = across_tp(state)
            (state_other,) = ring.close(state_other)

    pairs = [[(2 * source + half, 3 - half) for half in range(2)] for source in range(2)]
    arrived = [lax.ppermute(leave, ("segment", "tp"), pair) for pair in pairs]
    stay_came = lax.ppermute(stay, "segment", [(0, 1)])
    both = jnp.stack(
        [
            jnp.where(
                first_core,
                states[0],
                (stay_came + arrived[0].astype(jnp.float32)).astype(jnp.bfloat16),
            ),
            jnp.where(
                first_core,
                first_came,
                (stay + arrived[1].astype(jnp.float32)).astype(jnp.bfloat16),
            ),
        ]
    )
    return jnp.swapaxes(both, 1, 2)[None]


def solution(mesh):
    return jax.shard_map(
        per_device,
        mesh=mesh,
        in_specs=(
            P(None, "seq", "tp"),
            P(),
            P(),
            P("segment", None),
            P("segment", "seq", "tp"),
            P("segment", None, "tp"),
            P("segment", None, "tp"),
            P("segment", "tp", "seq"),
        ),
        out_specs=P("segment", None, "seq", "tp"),
        check_vma=False,
    )
```
